32 devices in a mesh: seq: 8 (over y, x, core), rep: 4 (over z).
Axes of the slice: x: 2, y: 2, z: 4, core: 2. Of those that a mesh axis runs over, the one named last changes fastest.
Arguments:
- signal: bfloat16 [4, 1024, 512], P('rep', 'seq'), may hold values from -6 to 6
- w_qkv: bfloat16 [512, 1536], P('seq'), may hold values from -0.25 to 0.25
- w_out: bfloat16 [512, 512], P('seq'), may hold values from -0.25 to 0.25
- offsets: int32 [2, 8], replicated, may hold values from 0 to 7, as said below
- d_result: bfloat16 [4, 1024, 512], P('rep', 'seq'), may hold values from -30 to 30
Outputs:
- result: bfloat16 [4, 1024, 512], P('rep', 'seq')
- d_signal: bfloat16 [4, 1024, 512], P('rep', 'seq')
- d_w_qkv: float32 [512, 1536], P('seq')
- d_w_out: float32 [512, 512], P('seq')
The draws below stay inside these ranges and needn't reach their ends.
Inputs may be any that keep to these rules, and one draw needn't show every extreme that they name: offsets[0, h] is head h's offset at the level of rate 8 and lies below 8; offsets[1, h] is its offset at the level of rate 8; in each row some head takes the row's top value.
All inputs are finite; a program needn't handle non-finite values.
Results may differ from the reference program's by a relative error of at most 0.0075.
The reference program's roundings to bfloat16 on the way count: a program that leaves them out, or rounds other values in their place, can miss the bound.
Values may be sent and summed in bfloat16 or wider, within the bound.
No kernel may reach another device: no remote copies, remote signals or barrier semaphores. Data moves between devices by JAX's collectives and lax.ppermute only.
A program may use at most 64 MiB of HBM per device.

```python
import math
import jax
import jax.numpy as jnp
from jax import lax

D = 512
HEADS = 8
T_DEV = 128
HD = 64
TOKENS = 1024
BATCH = 4
MID_RATE = 8
FAR_RATE = 8


def draw_offsets(key, part):
    keys_four = jax.random.split(jax.random.fold_in(key, 17), 4)
    mid_draw = jax.random.randint(keys_four[0], (HEADS,), 0, MID_RATE)
    far_draw = jax.random.randint(keys_four[1], (HEADS,), 0, FAR_RATE)
    mid_head = jax.random.randint(keys_four[2], (), 0, HEADS)
    far_head = jax.random.randint(keys_four[3], (), 0, HEADS)
    head_ids = jnp.arange(HEADS)
    mid_draw = jnp.where(head_ids == mid_head, MID_RATE - 1, mid_draw)
    far_draw = jnp.where(head_ids == far_head, FAR_RATE - 1, far_draw)
    return jnp.stack([mid_draw, far_draw]).astype(jnp.int32)


def draw_d_result(key, part):
    keys_two = jax.random.split(jax.random.fold_in(key, 29), 2)
    base_draw = jnp.clip(jax.random.normal(keys_two[0], (BATCH, TOKENS, D), jnp.float32), -6.0, 6.0)
    heavy_block = jax.random.randint(keys_two[1], (BATCH,), 0, TOKENS // T_DEV)
    block_ids = jnp.arange(TOKENS) // T_DEV
    factor = jnp.where(block_ids[None, :] == heavy_block[:, None], 5.0, 1.0).astype(jnp.float32)
    return (base_draw * factor[:, :, None]).astype(jnp.bfloat16)


def block_levels(own_key, shape, cuts, smallest, high):
    def one(axis_at, parts):
        steps = jax.random.uniform(jax.random.fold_in(jax.random.fold_in(own_key, 6), axis_at), (parts,), jnp.float32, smallest / len(cuts), high / len(cuts))
        return jnp.repeat(jnp.exp(steps), shape[axis_at] // parts).reshape((-1,) + (1,) * (len(shape) - axis_at - 1))

    loudness = one(*cuts[0])
    for cut in cuts[1:]:
        loudness = loudness * one(*cut)
    return loudness


def scatter_about(key, dims, deviation, limit, pieces=(), held_as=jnp.bfloat16):
    gain = block_levels(key, dims, pieces, -0.22, 0.18) if pieces else 1.0
    entries = jax.random.normal(key, dims, jnp.float32) * deviation * gain
    return jnp.minimum(jnp.maximum(entries, -limit), limit).astype(held_as)


def setup_inputs(seed: int = 0) -> dict:
    splits = jax.random.split(jax.random.key(seed), 6)
    signal = scatter_about(splits[0], (BATCH, TOKENS, D), 1.0, 6.0, ((0, 4), (1, 8)))
    w_qkv = scatter_about(splits[1], (D, 3 * D), D ** -0.5, 0.25, ((0, 8),))
    w_out = scatter_about(splits[2], (D, D), D ** -0.5, 0.25, ((0, 8),))
    offsets = draw_offsets(jax.random.fold_in(splits[5], 71), 0)
    d_result = draw_d_result(jax.random.fold_in(splits[5], 71), 0)
    return {"signal": signal, "w_qkv": w_qkv, "w_out": w_out, "offsets": offsets, "d_result": d_result}


def to_half(tensor):
    return lax.optimization_barrier(tensor.astype(jnp.bfloat16))

def normalize(tensor):
    widened = tensor.astype(jnp.float32)
    factor = lax.rsqrt(lax.optimization_barrier(jnp.mean(widened * widened, axis=-1, keepdims=True)) + 1e-06)
    return (widened * factor, factor)

def dilated_row_index(full_row_tensor, dilation_step, start_shift):
    row_total = full_row_tensor.shape[0] // dilation_step
    reshaped_tensor = full_row_tensor.reshape(row_total, dilation_step, full_row_tensor.shape[1], full_row_tensor.shape[2])
    chosen_rows_list = jnp.arange(dilation_step)[:, None] == start_shift[None, :]
    kept_rows = jnp.where(chosen_rows_list[None, :, :, None], reshaped_tensor, jnp.zeros((), full_row_tensor.dtype))
    return lax.optimization_barrier(jnp.sum(kept_rows, axis=1))

def scatter_row_subset(gathered_rows, dilation_step, start_shift):
    row_total, head_total, feature_count = gathered_rows.shape
    chosen_rows_list = jnp.arange(dilation_step)[:, None] == start_shift[None, :]
    scattered_rows = jnp.where(chosen_rows_list[None, :, :, None], gathered_rows[:, None], jnp.zeros((), gathered_rows.dtype))
    return scattered_rows.reshape(row_total * dilation_step, head_total, feature_count)

def dilation_level_forward(q_sel, k_sel, v_sel, segment_count, logit_scale):
    head_total, head_dim = (q_sel.shape[1], q_sel.shape[2])
    q_four = q_sel.astype(jnp.float32).reshape(segment_count, -1, head_total, head_dim)
    k_four = k_sel.astype(jnp.float32).reshape(segment_count, -1, head_total, head_dim)
    v_four = v_sel.astype(jnp.float32).reshape(segment_count, -1, head_total, head_dim)
    scores = jnp.einsum('smhd,snhd->shmn', q_four, k_four) * logit_scale
    exp_scores = jnp.exp(scores)
    softmax_denominator = lax.optimization_barrier(jnp.sum(exp_scores, axis=-1))
    softmax_numerator = jnp.einsum('shmn,snhd->smhd', to_half(exp_scores).astype(jnp.float32), v_four)
    softmax_denominator = jnp.transpose(softmax_denominator, (0, 2, 1)).reshape(-1, head_total)
    return (softmax_numerator.reshape(-1, head_total, head_dim), softmax_denominator)

def dilation_level_backward(q_sel, k_sel, v_sel, g_sel, delta_sel, picked_denominator, segment_count, logit_scale):
    head_total, head_dim = (q_sel.shape[1], q_sel.shape[2])
    q_four = q_sel.astype(jnp.float32).reshape(segment_count, -1, head_total, head_dim)
    k_four = k_sel.astype(jnp.float32).reshape(segment_count, -1, head_total, head_dim)
    v_four = v_sel.astype(jnp.float32).reshape(segment_count, -1, head_total, head_dim)
    g_four = g_sel.astype(jnp.float32).reshape(segment_count, -1, head_total, head_dim)
    delta_four = jnp.transpose(delta_sel.reshape(segment_count, -1, head_total), (0, 2, 1))
    denom_four = jnp.transpose(picked_denominator.reshape(segment_count, -1, head_total), (0, 2, 1))
    scores = jnp.einsum('smhd,snhd->shmn', q_four, k_four) * logit_scale
    prob_full = jnp.exp(scores) / denom_four[..., None]
    prob_half = to_half(prob_full).astype(jnp.float32)
    value_gradient = jnp.einsum('shmn,smhd->snhd', prob_half, g_four)
    probability_gradient = jnp.einsum('smhd,snhd->shmn', g_four, v_four)
    score_gradient = to_half(prob_full * (probability_gradient - delta_four[..., None])).astype(jnp.float32)
    d_query = jnp.einsum('shmn,snhd->smhd', score_gradient, k_four) * logit_scale
    d_key = jnp.einsum('shmn,smhd->snhd', score_gradient, q_four) * logit_scale
    return (d_query.reshape(-1, head_total, head_dim), d_key.reshape(-1, head_total, head_dim), value_gradient.reshape(-1, head_total, head_dim))

def one_window(signal_rows, w_qkv, w_out, offsets, upstream):
    length = signal_rows.shape[0]
    logit_scale = 1.0 / math.sqrt(HD)
    qkv_rows = to_half(jnp.dot(signal_rows, w_qkv, preferred_element_type=jnp.float32))
    query_rows = qkv_rows[:, :D].reshape(length, HEADS, HD)
    key_matrix_rows = qkv_rows[:, D:2 * D].reshape(length, HEADS, HD)
    value_matrix_rows = qkv_rows[:, 2 * D:].reshape(length, HEADS, HD)
    q_wide, q_factor = normalize(query_rows)
    k_wide, k_factor = normalize(key_matrix_rows)
    query_normalized = to_half(q_wide)
    key_normalized = to_half(k_wide)
    dilation_levels = [(1, jnp.zeros((HEADS,), jnp.int32), T_DEV), (MID_RATE, offsets[0], MID_RATE * T_DEV), (FAR_RATE, offsets[1], TOKENS)]
    softmax_numerator = jnp.zeros((length, HEADS, HD), jnp.float32)
    softmax_denominator = jnp.zeros((length, HEADS), jnp.float32)
    for dilation_step, start_shift, segment_length in dilation_levels:
        segment_count = length // segment_length
        picked_numerator, picked_denominator = dilation_level_forward(dilated_row_index(query_normalized, dilation_step, start_shift), dilated_row_index(key_normalized, dilation_step, start_shift), dilated_row_index(value_matrix_rows, dilation_step, start_shift), segment_count, logit_scale)
        softmax_numerator = softmax_numerator + scatter_row_subset(picked_numerator, dilation_step, start_shift)
        softmax_denominator = softmax_denominator + scatter_row_subset(picked_denominator[..., None], dilation_step, start_shift)[..., 0]
    attn_three = to_half(softmax_numerator / softmax_denominator[..., None])
    attn_rows = attn_three.reshape(length, D)
    result = to_half(jnp.dot(attn_rows, w_out, preferred_element_type=jnp.float32))
    attention_gradient = to_half(jnp.dot(upstream, w_out.T, preferred_element_type=jnp.float32)).reshape(length, HEADS, HD)
    correction_rows = lax.optimization_barrier(jnp.sum(attention_gradient.astype(jnp.float32) * attn_three.astype(jnp.float32), axis=-1))
    normed_query_gradient = jnp.zeros((length, HEADS, HD), jnp.float32)
    normed_key_gradient = jnp.zeros((length, HEADS, HD), jnp.float32)
    value_gradient = jnp.zeros((length, HEADS, HD), jnp.float32)
    for dilation_step, start_shift, segment_length in dilation_levels:
        segment_count = length // segment_length
        gradient_list = dilation_level_backward(dilated_row_index(query_normalized, dilation_step, start_shift), dilated_row_index(key_normalized, dilation_step, start_shift), dilated_row_index(value_matrix_rows, dilation_step, start_shift), dilated_row_index(attention_gradient, dilation_step, start_shift), dilated_row_index(correction_rows[..., None], dilation_step, start_shift)[..., 0], dilated_row_index(softmax_denominator[..., None], dilation_step, start_shift)[..., 0], segment_count, logit_scale)
        normed_query_gradient = normed_query_gradient + scatter_row_subset(gradient_list[0], dilation_step, start_shift)
        normed_key_gradient = normed_key_gradient + scatter_row_subset(gradient_list[1], dilation_step, start_shift)
        value_gradient = value_gradient + scatter_row_subset(gradient_list[2], dilation_step, start_shift)
    d_query = q_factor * (normed_query_gradient - q_wide * lax.optimization_barrier(jnp.mean(normed_query_gradient * q_wide, axis=-1, keepdims=True)))
    d_key = k_factor * (normed_key_gradient - k_wide * lax.optimization_barrier(jnp.mean(normed_key_gradient * k_wide, axis=-1, keepdims=True)))
    d_qkv = to_half(jnp.concatenate([d_query.reshape(length, D), d_key.reshape(length, D), value_gradient.reshape(length, D)], axis=1))
    d_signal = to_half(jnp.dot(d_qkv, w_qkv.T, preferred_element_type=jnp.float32))
    grad_qkv = jnp.dot(signal_rows.T, d_qkv, preferred_element_type=jnp.float32)
    grad_out = jnp.dot(attn_rows.T, upstream, preferred_element_type=jnp.float32)
    return (result, d_signal, grad_qkv, grad_out)

def reference(signal, w_qkv, w_out, offsets, d_result):
    results = []
    d_signals = []
    grad_qkv = jnp.zeros((D, 3 * D), jnp.float32)
    grad_out = jnp.zeros((D, D), jnp.float32)
    for win_index in range(BATCH):
        outputs = one_window(signal[win_index], w_qkv, w_out, offsets, d_result[win_index])
        results.append(outputs[0])
        d_signals.append(outputs[1])
        grad_qkv = grad_qkv + outputs[2]
        grad_out = grad_out + outputs[3]
    return (jnp.stack(results), jnp.stack(d_signals), grad_qkv, grad_out)
```

```python
import math

import jax
import jax.numpy as jnp
from jax import lax
from jax.experimental import pallas as pl
from jax.experimental.pallas import tpu as pltpu
from jax.sharding import PartitionSpec as P

HEADS = 8


def from_partner(value, axis, stride):
    mask = 2**stride
    pairs = [(source, source ^ mask) for source in range(lax.axis_size(axis))]
    return lax.ppermute(value, axis, pairs)


def normalize(tensor):
    widened = tensor.astype(jnp.float32)
    factor = lax.rsqrt(jnp.mean(widened * widened, axis=-1, keepdims=True) + 1e-06)
    return (widened * factor, factor)


def gather_row_subset(full_row_tensor, dilation_step, start_shift):
    row_total = full_row_tensor.shape[0] // dilation_step
    reshaped_tensor = full_row_tensor.reshape(
        row_total, dilation_step, full_row_tensor.shape[1], full_row_tensor.shape[2]
    )
    chosen_rows_list = jnp.arange(dilation_step)[:, None] == start_shift[None, :]
    kept_rows = jnp.where(
        chosen_rows_list[None, :, :, None], reshaped_tensor, jnp.zeros((), full_row_tensor.dtype)
    )
    return jnp.sum(kept_rows, axis=1)


def scatter_row_subset(gathered_rows, dilation_step, start_shift):
    row_total, head_total, feature_count = gathered_rows.shape
    chosen_rows_list = jnp.arange(dilation_step)[:, None] == start_shift[None, :]
    scattered_rows = jnp.where(
        chosen_rows_list[None, :, :, None],
        gathered_rows[:, None],
        jnp.zeros((), gathered_rows.dtype),
    )
    return scattered_rows.reshape(row_total * dilation_step, head_total, feature_count)


def join_halves(own_part, peer_part, upper_bit):
    return jnp.where(
        upper_bit == 1,
        jnp.concatenate([peer_part, own_part], axis=0),
        jnp.concatenate([own_part, peer_part], axis=0),
    )


def attend(query_matrix, key_matrix_rows, value_matrix_rows, logit_scale):
    scores = (
        jnp.einsum(
            "ryk,oyk->yro", query_matrix, key_matrix_rows, preferred_element_type=jnp.float32
        )
        * logit_scale
    )
    exp_scores = jnp.exp(scores)
    softmax_denominator = jnp.sum(exp_scores, axis=-1).T
    softmax_numerator = jnp.einsum(
        "tcg,gto->cto",
        exp_scores.astype(jnp.bfloat16),
        value_matrix_rows,
        preferred_element_type=jnp.float32,
    )
    return (softmax_numerator, softmax_denominator)


def attend_back(
    query_matrix,
    key_matrix_rows,
    value_matrix_rows,
    gradient_rows,
    correction_rows,
    denom_rows,
    logit_scale,
):
    scores = (
        jnp.einsum(
            "ryk,oyk->yro", query_matrix, key_matrix_rows, preferred_element_type=jnp.float32
        )
        * logit_scale
    )
    prob_full = jnp.exp(scores) / denom_rows.T[:, :, None]
    value_gradient = jnp.einsum(
        "jvy,vjk->yjk",
        prob_full.astype(jnp.bfloat16),
        gradient_rows,
        preferred_element_type=jnp.float32,
    )
    probability_gradient = jnp.einsum(
        "ryk,oyk->yro", gradient_rows, value_matrix_rows, preferred_element_type=jnp.float32
    )
    score_gradient = (prob_full * (probability_gradient - correction_rows.T[:, :, None])).astype(
        jnp.bfloat16
    )
    d_query = (
        jnp.einsum(
            "tcg,gto->cto", score_gradient, key_matrix_rows, preferred_element_type=jnp.float32
        )
        * logit_scale
    )
    d_key = (
        jnp.einsum("jvy,vjk->yjk", score_gradient, query_matrix, preferred_element_type=jnp.float32)
        * logit_scale
    )
    return (d_query, d_key, value_gradient)


def local(signal, w_qkv, w_out, offsets, d_result):
    tok_rows = signal[0]
    upstream = d_result[0]
    t_dev, model_dim = tok_rows.shape
    head_total = HEADS
    head_dim = model_dim // head_total
    logit_scale = 1.0 / math.sqrt(head_dim)
    shards = lax.axis_size("seq")
    mid_rate = min(16, shards)
    mid_bits = mid_rate.bit_length() - 1
    shard_index = lax.axis_index("seq")
    mid_off = offsets[0]
    far_off = offsets[1]
    qkv_full, out_full = (
        lax.all_gather(w_qkv, "seq", axis=0, tiled=True),
        lax.all_gather(w_out, "seq", axis=0, tiled=True),
    )
    projected = jnp.dot(tok_rows, qkv_full, preferred_element_type=jnp.float32)
    qkv_rows = projected.astype(jnp.bfloat16)
    query_rows = qkv_rows[:, :model_dim].reshape(t_dev, head_total, head_dim)
    key_matrix_rows = qkv_rows[:, model_dim : 2 * model_dim].reshape(t_dev, head_total, head_dim)
    value_matrix_rows = qkv_rows[:, 2 * model_dim :].reshape(t_dev, head_total, head_dim)
    q_wide, q_factor = normalize(query_rows)
    k_wide, k_factor = normalize(key_matrix_rows)
    query_normalized = q_wide.astype(jnp.bfloat16)
    key_normalized = k_wide.astype(jnp.bfloat16)
    numer_near, denom_near = attend(
        query_normalized, key_normalized, value_matrix_rows, logit_scale
    )
    key_value = jnp.concatenate([key_normalized, value_matrix_rows], axis=2)
    mid_local = gather_row_subset(key_value, mid_rate, mid_off)
    far_local = gather_row_subset(key_value, shards, far_off)
    mid_all = mid_local
    for bit_num in range(mid_bits):
        partner = from_partner(mid_all, "seq", bit_num)
        mid_all = join_halves(mid_all, partner, shard_index // (1 << bit_num) % 2)
    far_all = lax.all_gather(far_local, "seq", axis=0, tiled=True)
    mid_keys_all = mid_all[..., :head_dim]
    mid_vals_all = mid_all[..., head_dim:]
    far_keys_all = far_all[..., :head_dim]
    far_vals_all = far_all[..., head_dim:]
    q_mid = gather_row_subset(query_normalized, mid_rate, mid_off)
    q_far = gather_row_subset(query_normalized, shards, far_off)
    numer_mid, denom_mid = attend(q_mid, mid_keys_all, mid_vals_all, logit_scale)
    numer_far, denom_far = attend(q_far, far_keys_all, far_vals_all, logit_scale)
    softmax_numerator = (
        numer_near
        + scatter_row_subset(numer_mid, mid_rate, mid_off)
        + scatter_row_subset(numer_far, shards, far_off)
    )
    softmax_denominator = (
        denom_near
        + scatter_row_subset(denom_mid[..., None], mid_rate, mid_off)[..., 0]
        + scatter_row_subset(denom_far[..., None], shards, far_off)[..., 0]
    )
    attn_three = (softmax_numerator / softmax_denominator[..., None]).astype(jnp.bfloat16)
    attn_rows = attn_three.reshape(t_dev, model_dim)
    layer_out = jnp.dot(attn_rows, out_full, preferred_element_type=jnp.float32)
    d_attn_wide = jnp.dot(upstream, out_full.T, preferred_element_type=jnp.float32)
    result = layer_out.astype(jnp.bfloat16)
    attention_gradient = d_attn_wide.astype(jnp.bfloat16).reshape(t_dev, head_total, head_dim)
    correction_rows = jnp.sum(
        attention_gradient.astype(jnp.float32) * attn_three.astype(jnp.float32), axis=-1
    )
    dq_near, dk_near, dv_near = attend_back(
        query_normalized,
        key_normalized,
        value_matrix_rows,
        attention_gradient,
        correction_rows,
        softmax_denominator,
        logit_scale,
    )
    g_mid = gather_row_subset(attention_gradient, mid_rate, mid_off)
    g_far = gather_row_subset(attention_gradient, shards, far_off)
    delta_mid = gather_row_subset(correction_rows[..., None], mid_rate, mid_off)[..., 0]
    delta_far = gather_row_subset(correction_rows[..., None], shards, far_off)[..., 0]
    denom_mid_q = gather_row_subset(softmax_denominator[..., None], mid_rate, mid_off)[..., 0]
    denom_far_q = gather_row_subset(softmax_denominator[..., None], shards, far_off)[..., 0]
    dq_mid, dk_mid_part, dv_mid_part = attend_back(
        q_mid, mid_keys_all, mid_vals_all, g_mid, delta_mid, denom_mid_q, logit_scale
    )
    dq_far, dk_far_part, dv_far_part = attend_back(
        q_far, far_keys_all, far_vals_all, g_far, delta_far, denom_far_q, logit_scale
    )
    query_pack = jnp.concatenate([q_mid, g_mid], axis=2)
    stat_pack = jnp.stack([delta_mid, denom_mid_q], axis=2)
    for bit_num in range(mid_bits):
        upper_bit = shard_index // (1 << bit_num) % 2
        peer_query = from_partner(query_pack, "seq", bit_num)
        peer_stats = from_partner(stat_pack, "seq", bit_num)
        query_pack = join_halves(query_pack, peer_query, upper_bit)
        stat_pack = join_halves(stat_pack, peer_stats, upper_bit)
    unused_mid, dk_mid, dv_mid = attend_back(
        query_pack[..., :head_dim],
        mid_local[..., :head_dim],
        mid_local[..., head_dim:],
        query_pack[..., head_dim:],
        stat_pack[..., 0],
        stat_pack[..., 1],
        logit_scale,
    )
    far_query_pack = lax.all_gather(
        jnp.concatenate([q_far, g_far], axis=2), "seq", axis=0, tiled=True
    )
    far_stat_pack = lax.all_gather(
        jnp.stack([delta_far, denom_far_q], axis=2), "seq", axis=0, tiled=True
    )
    unused_far, dk_far, dv_far = attend_back(
        far_query_pack[..., :head_dim],
        far_local[..., :head_dim],
        far_local[..., head_dim:],
        far_query_pack[..., head_dim:],
        far_stat_pack[..., 0],
        far_stat_pack[..., 1],
        logit_scale,
    )
    normed_query_gradient = (
        dq_near
        + scatter_row_subset(dq_mid, mid_rate, mid_off)
        + scatter_row_subset(dq_far, shards, far_off)
    )
    normed_key_gradient = (
        dk_near
        + scatter_row_subset(dk_mid, mid_rate, mid_off)
        + scatter_row_subset(dk_far, shards, far_off)
    )
    value_gradient = (
        dv_near
        + scatter_row_subset(dv_mid, mid_rate, mid_off)
        + scatter_row_subset(dv_far, shards, far_off)
    )
    d_query = q_factor * (
        normed_query_gradient
        - q_wide * jnp.mean(normed_query_gradient * q_wide, axis=-1, keepdims=True)
    )
    d_key = k_factor * (
        normed_key_gradient
        - k_wide * jnp.mean(normed_key_gradient * k_wide, axis=-1, keepdims=True)
    )
    d_qkv = jnp.concatenate(
        [
            d_query.reshape(t_dev, model_dim),
            d_key.reshape(t_dev, model_dim),
            value_gradient.reshape(t_dev, model_dim),
        ],
        axis=1,
    ).astype(jnp.bfloat16)
    d_input = jnp.dot(d_qkv, qkv_full.T, preferred_element_type=jnp.float32)
    d_signal = d_input.astype(jnp.bfloat16)
    grad_in = jnp.einsum("ti,tj->ij", tok_rows, d_qkv, preferred_element_type=jnp.float32)
    grad_mix = jnp.einsum("ti,tj->ij", attn_rows, upstream, preferred_element_type=jnp.float32)
    owned = lax.psum_scatter(
        jnp.concatenate([grad_in, grad_mix], axis=1), "seq", scatter_dimension=0, tiled=True
    )
    owned = lax.psum(owned, "rep")
    return (result[None], d_signal[None], owned[:, : 3 * model_dim], owned[:, 3 * model_dim :])


BF = jnp.bfloat16
F32 = jnp.float32
TD = 128
HD = 64
DM = 512
NN = (((1,), (0,)), ((), ()))
NT = (((1,), (1,)), ((), ()))
TN = (((0,), (0,)), ((), ()))


def mm(a, b, dims=NN):
    return lax.dot_general(a, b, dims, preferred_element_type=F32)


def low_lanes(rows):
    return lax.broadcasted_iota(jnp.int32, (rows, 128), 1) < HD


def swap_halves(tile):
    return pltpu.roll(tile.astype(F32), HD, 1)


def half_ones():
    a = lax.broadcasted_iota(jnp.int32, (128, 128), 0) < HD
    b = lax.broadcasted_iota(jnp.int32, (128, 128), 1) < HD
    return (a == b).astype(BF)


def half_means(values, ones):
    head = values.astype(BF)
    tail = (values - head.astype(F32)).astype(BF)
    return (mm(head, ones) + mm(tail, ones)) * (1.0 / HD)


def pack_kernel(sig_ref, wqkv_ref, wout_ref, pay0, pay1, pay2, pay3, wrow_ref):
    chip = lax.axis_index("seq") // 2
    low = low_lanes(HD)
    for t in range(4):
        q = wqkv_ref[:, 128 * t : 128 * t + 128].astype(F32)
        k = wqkv_ref[:, DM + 128 * t : DM + 128 * t + 128].astype(F32)
        wrow_ref[:, 256 * t : 256 * t + 128] = jnp.where(low, q, swap_halves(k)).astype(BF)
        wrow_ref[:, 256 * t + 128 : 256 * t + 256] = jnp.where(low, swap_halves(q), k).astype(BF)
    wrow_ref[:, 2 * DM : 3 * DM] = wqkv_ref[:, 2 * DM : 3 * DM]
    wrow_ref[:, 3 * DM : 4 * DM] = wout_ref[...]
    for t, pay in enumerate((pay0, pay1, pay2, pay3)):
        other = chip ^ t
        pay[0:TD, :] = sig_ref[...]
        pay[TD:, 0:256] = wrow_ref[:, pl.ds(pl.multiple_of(other * 256, 256), 256)]
        pay[TD:, 256:384] = wrow_ref[:, pl.ds(pl.multiple_of(2 * DM + other * 128, 128), 128)]
        pay[TD:, 384:512] = jnp.zeros((HD, 128), BF)


def head_kernel(off_ref, *refs):
    S, D, wo_ref = refs[0:8], refs[8:16], refs[16]
    out, gout_ref = refs[17:25], refs[25]
    w_scr, qk_scr, v_scr, acc_scr, e_scr, g_scr, dqk_scr, dv_scr, rho_scr, qkw_scr, dw_scr = refs[26:]
    me = lax.axis_index("seq")
    core = me % 2
    scale = 1.0 / math.sqrt(HD)
    low = low_lanes(TD)
    ones = half_ones()
    for m in range(8):
        rows = pl.ds(pl.multiple_of((me ^ m) * HD, HD), HD)
        w_scr[rows, 0:128] = S[m][TD:, pl.ds(pl.multiple_of(core * 128, 128), 128)]
        w_scr[rows, 128:256] = S[m][TD:, 256:384]

    def forward(qkn, vv):
        flipped = swap_halves(qkn)
        qn = qkn[:, :HD].astype(BF)
        kn = flipped[:, :HD].astype(BF)
        e = jnp.exp(mm(qn, kn, NT) * scale)
        den = jnp.sum(e, axis=1, keepdims=True)
        num = mm(e.astype(BF), vv.astype(BF))
        return e, jnp.where(low, num, den)

    def backward(e, qkn, vv, grads, den):
        flipped = swap_halves(qkn)
        kz = jnp.where(low, flipped, 0.0).astype(BF)
        qz = jnp.where(low, 0.0, flipped).astype(BF)
        da = jnp.where(low, grads, 0.0).astype(BF)
        delta = grads[:, HD : HD + 1]
        prob = e * (1.0 / den)
        dv = mm(prob.astype(BF), da, TN)
        dp = mm(da, vv.astype(BF), NT)
        ds = (prob * (dp - delta)).astype(BF)
        return mm(ds, kz) + mm(ds, qz, TN), dv

    for m in range(8):
        rows = slice(TD * m, TD * m + TD)
        qkv = mm(S[m][0:TD, :], w_scr[...]).astype(BF).astype(F32)
        qk = qkv[:, 0:128]
        pair = qkv[:, 128:256]
        vv = jnp.where(core == 1, swap_halves(pair), pair)
        rho = lax.rsqrt(half_means(qk * qk, ones) + 1e-6)
        qkw = qk * rho
        qkn = qkw.astype(BF).astype(F32)
        qkw_scr[rows, :] = qkw
        rho_scr[rows, :] = rho
        qk_scr[rows, :] = qkn
        v_scr[rows, :] = vv
        e, val = forward(qkn, vv)
        e_scr[m] = e
        acc_scr[rows, :] = val
    picks = [pl.ds(off_ref[level, me], TD, stride=8) for level in range(2)]
    for level, pick in enumerate(picks):
        e, val = forward(qk_scr[pick, :], v_scr[pick, :])
        e_scr[8 + level] = e
        acc_scr[pick, :] = acc_scr[pick, :] + val

    wide = jnp.concatenate([wo_ref[...], jnp.zeros((HD, DM), BF)], axis=0)
    for m in range(8):
        rows = slice(TD * m, TD * m + TD)
        acc = acc_scr[rows, :]
        attn = jnp.where(low, acc / swap_halves(acc), 0.0).astype(BF)
        da = mm(D[m][...], wide, NT).astype(BF).astype(F32)
        delta = jnp.sum(da * attn.astype(F32), axis=1, keepdims=True)
        grads = jnp.where(low, da, delta)
        g_scr[rows, :] = grads
        part = mm(attn, D[m][...], TN)
        gout = part if m == 0 else gout + part
        dqk, dv = backward(e_scr[m], qk_scr[rows, :], v_scr[rows, :], grads, acc[:, HD : HD + 1])
        dqk_scr[rows, :] = dqk
        dv_scr[rows, :] = jnp.where(low, dv, swap_halves(attn))
    gout_ref[...] = gout[:HD, :].astype(BF)
    for level, pick in enumerate(picks):
        dqk, dv = backward(
            e_scr[8 + level],
            qk_scr[pick, :],
            v_scr[pick, :],
            g_scr[pick, :],
            acc_scr[pick, :][:, HD : HD + 1],
        )
        dqk_scr[pick, :] = dqk_scr[pick, :] + dqk
        dv_scr[pick, :] = dv_scr[pick, :] + jnp.where(low, dv, 0.0)

    for m in range(8):
        rows = slice(TD * m, TD * m + TD)
        dqk = dqk_scr[rows, :] * scale
        qkw = qkw_scr[rows, :]
        dqk = rho_scr[rows, :] * (dqk - qkw * half_means(dqk * qkw, ones))
        out[m][0:TD, 0:128] = dqk.astype(BF)
        out[m][0:TD, 128:256] = dv_scr[rows, :].astype(BF)
        part = mm(S[m][0:TD, :], out[m][0:TD, :], TN)
        if m == 0:
            dw_scr[...] = part
        else:
            dw_scr[...] = dw_scr[...] + part
    for m in range(8):
        rows = pl.ds(pl.multiple_of((me ^ m) * HD, HD), HD)
        out[m][TD:, :] = dw_scr[rows, :].astype(BF)


def regroup_kernel(*refs):
    R, gout_ref, z_ref = refs[0:8], refs[8], refs[9]
    low = low_lanes(HD)
    for m in range(8):
        z_ref[:, 128 * m : 128 * m + 128] = R[m][TD:, 0:128]
    for t in range(4):
        a = R[2 * t][TD:, 128:256].astype(F32)
        b = swap_halves(R[2 * t + 1][TD:, 128:256])
        z_ref[:, 2 * DM + 128 * t : 2 * DM + 128 * t + 128] = jnp.where(low, a, b).astype(BF)
    z_ref[:, 3 * DM :] = gout_ref[...]


def owner_kernel(*refs):
    R, G = refs[0:8], refs[8:16]
    res_ref, dsig_ref, w_scr, wo_scr, d_scr, a_scr = refs[16:]
    me = lax.axis_index("seq")
    chip, core = me // 2, me % 2
    low = low_lanes(TD)
    for m in range(8):
        w_scr[pl.ds(pl.multiple_of((me ^ m) * HD, HD), HD), :] = G[m][:, 0 : 3 * DM]
        wo_scr[HD * m : HD * m + HD, :] = G[m][:, 3 * DM :]
        d_scr[:, pl.ds(pl.multiple_of((me ^ m) * 128, 128), 128)] = R[m][0:TD, 0:128]
    for t in range(4):
        a = R[2 * t][0:TD, 128:256].astype(F32)
        b = R[2 * t + 1][0:TD, 128:256].astype(F32)
        a_scr[:, 128 * t : 128 * t + 128] = jnp.where(low, swap_halves(a), b).astype(BF)
        even = jnp.where(core == 1, b, a)
        odd = jnp.where(core == 1, a, b)
        col = pl.multiple_of(2 * DM + (chip ^ t) * 128, 128)
        d_scr[:, pl.ds(col, 128)] = jnp.where(low, even, swap_halves(odd)).astype(BF)
    res_ref[...] = mm(a_scr[...], wo_scr[...]).astype(BF)
    dsig_ref[...] = mm(d_scr[...], w_scr[...], NT).astype(BF)


def total_kernel(*refs):
    Z, dw_ref, dwo_ref = refs[:-2], refs[-2], refs[-1]
    me = lax.axis_index("seq")
    chip, core = me // 2, me % 2
    low = low_lanes(HD)

    def tile(start):
        total = Z[0][:, start : start + 128].astype(F32)
        for z in Z[1:]:
            total = total + z[:, start : start + 128].astype(F32)
        return total

    for t in range(4):
        a, b = tile(256 * t), tile(256 * t + 128)
        even = jnp.where(core == 1, b, a)
        odd = jnp.where(core == 1, a, b)
        col = (chip ^ t) * 128
        dw_ref[:, pl.ds(pl.multiple_of(col, 128), 128)] = jnp.where(low, even, swap_halves(odd))
        dw_ref[:, pl.ds(pl.multiple_of(DM + col, 128), 128)] = jnp.where(
            low, swap_halves(even), odd
        )
        v = tile(2 * DM + 128 * t)
        dw_ref[:, pl.ds(pl.multiple_of(2 * DM + col, 128), 128)] = jnp.where(
            core == 1, swap_halves(v), v
        )
        dwo_ref[:, 128 * t : 128 * t + 128] = tile(3 * DM + 128 * t)


def vmem_call(body, ins, outs, scratch=(), flops=0, smem=0):
    bytes_moved = sum(x.size * x.dtype.itemsize for x in list(ins) + list(outs))
    vmem = pl.BlockSpec(memory_space=pltpu.VMEM)
    return pl.pallas_call(
        body,
        out_shape=list(outs),
        in_specs=[pl.BlockSpec(memory_space=pltpu.SMEM)] * smem + [vmem] * (len(ins) - smem),
        out_specs=[vmem] * len(outs),
        scratch_shapes=list(scratch),
        compiler_params=pltpu.CompilerParams(vmem_limit_bytes=40 << 20),
        cost_estimate=pl.CostEstimate(flops=flops, bytes_accessed=bytes_moved, transcendentals=0),
    )(*ins)


def swap(value, mask, axis):
    return lax.ppermute(value, axis, [(i, i ^ mask) for i in range(lax.axis_size(axis))])


def shape(rows, cols, dtype=BF):
    return jax.ShapeDtypeStruct((rows, cols), dtype)


def spread(parts):
    out = [None] * 8
    for t in range(4):
        out[2 * t] = parts[t] if t == 0 else swap(parts[t], 2 * t, "seq")
    for t in range(4):
        out[2 * t + 1] = swap(out[2 * t], 1, "seq")
    return out


def local_heads(signal, w_qkv, w_out, offsets, d_result):
    sig, grad = signal[0], d_result[0]
    pays = vmem_call(
        pack_kernel,
        (sig, w_qkv, w_out),
        [shape(TD + HD, DM)] * 4 + [shape(HD, 4 * DM)],
    )
    wrow = pays[4]
    S = spread(pays[:4])
    D = spread([grad] * 4)
    G = spread([wrow] * 4)
    scr = [pltpu.VMEM((1024, 128), F32)]
    res = vmem_call(
        head_kernel,
        (offsets, *S, *D, w_out),
        [shape(TD + HD, 256)] * 8 + [shape(HD, DM)],
        scratch=[pltpu.VMEM((DM, 256), BF)]
        + scr * 3
        + [pltpu.VMEM((10, TD, TD), F32)]
        + scr * 5
        + [pltpu.VMEM((DM, 256), F32)],
        flops=10**9,
        smem=1,
    )
    P_out, gout = res[:8], res[8]
    R = [P_out[0]] + [swap(P_out[m], m, "seq") for m in range(1, 8)]
    (Z,) = vmem_call(regroup_kernel, (*R, gout), [shape(HD, 4 * DM)])
    reps = lax.axis_size("rep")
    Zs = [Z] + [swap(Z, m, "rep") for m in range(1, reps)]
    result, d_signal = vmem_call(
        owner_kernel,
        (*R, *G),
        [shape(TD, DM)] * 2,
        scratch=[
            pltpu.VMEM((DM, 3 * DM), BF),
            pltpu.VMEM((DM, DM), BF),
            pltpu.VMEM((TD, 3 * DM), BF),
            pltpu.VMEM((TD, DM), BF),
        ],
        flops=3 * 10**8,
    )
    dw, dwo = vmem_call(total_kernel, Zs, [shape(HD, 3 * DM, F32), shape(HD, DM, F32)])
    return (result[None], d_signal[None], dw, dwo)


def solution(mesh):
    in_specs = (P("rep", "seq", None), P("seq", None), P("seq", None), P(), P("rep", "seq", None))
    out_specs = (P("rep", "seq", None), P("rep", "seq", None), P("seq", None), P("seq", None))

    def body(signal, w_qkv, w_out, offsets, d_result):
        reps = mesh.shape["rep"]
        per_head = mesh.shape["seq"] == HEADS and reps & (reps - 1) == 0
        if per_head and signal.shape == (1, TD, DM) and w_qkv.shape == (HD, 3 * DM):
            return local_heads(signal, w_qkv, w_out, offsets, d_result)
        return local(signal, w_qkv, w_out, offsets, d_result)

    return jax.shard_map(body, mesh=mesh, in_specs=in_specs, out_specs=out_specs, check_vma=False)
```

```python
import functools
import math

import jax
import jax.numpy as jnp
from jax import lax
from jax.experimental import pallas as pl
from jax.experimental.pallas import tpu as pltpu
from jax.sharding import PartitionSpec as P

HEADS = 8


def from_partner(value, axis, stride):
    mask = 2**stride
    pairs = [(source, source ^ mask) for source in range(lax.axis_size(axis))]
    return lax.ppermute(value, axis, pairs)


def normalize(tensor):
    widened = tensor.astype(jnp.float32)
    factor = lax.rsqrt(jnp.mean(widened * widened, axis=-1, keepdims=True) + 1e-06)
    return (widened * factor, factor)


def gather_row_subset(full_row_tensor, dilation_step, start_shift):
    row_total = full_row_tensor.shape[0] // dilation_step
    reshaped_tensor = full_row_tensor.reshape(
        row_total, dilation_step, full_row_tensor.shape[1], full_row_tensor.shape[2]
    )
    chosen_rows_list = jnp.arange(dilation_step)[:, None] == start_shift[None, :]
    kept_rows = jnp.where(
        chosen_rows_list[None, :, :, None], reshaped_tensor, jnp.zeros((), full_row_tensor.dtype)
    )
    return jnp.sum(kept_rows, axis=1)


def scatter_row_subset(gathered_rows, dilation_step, start_shift):
    row_total, head_total, feature_count = gathered_rows.shape
    chosen_rows_list = jnp.arange(dilation_step)[:, None] == start_shift[None, :]
    scattered_rows = jnp.where(
        chosen_rows_list[None, :, :, None],
        gathered_rows[:, None],
        jnp.zeros((), gathered_rows.dtype),
    )
    return scattered_rows.reshape(row_total * dilation_step, head_total, feature_count)


def join_halves(own_part, peer_part, upper_bit):
    return jnp.where(
        upper_bit == 1,
        jnp.concatenate([peer_part, own_part], axis=0),
        jnp.concatenate([own_part, peer_part], axis=0),
    )


def attend(query_matrix, key_matrix_rows, value_matrix_rows, logit_scale):
    scores = (
        jnp.einsum(
            "ryk,oyk->yro", query_matrix, key_matrix_rows, preferred_element_type=jnp.float32
        )
        * logit_scale
    )
    exp_scores = jnp.exp(scores)
    softmax_denominator = jnp.sum(exp_scores, axis=-1).T
    softmax_numerator = jnp.einsum(
        "tcg,gto->cto",
        exp_scores.astype(jnp.bfloat16),
        value_matrix_rows,
        preferred_element_type=jnp.float32,
    )
    return (softmax_numerator, softmax_denominator)


def attend_back(
    query_matrix,
    key_matrix_rows,
    value_matrix_rows,
    gradient_rows,
    correction_rows,
    denom_rows,
    logit_scale,
):
    scores = (
        jnp.einsum(
            "ryk,oyk->yro", query_matrix, key_matrix_rows, preferred_element_type=jnp.float32
        )
        * logit_scale
    )
    prob_full = jnp.exp(scores) / denom_rows.T[:, :, None]
    value_gradient = jnp.einsum(
        "jvy,vjk->yjk",
        prob_full.astype(jnp.bfloat16),
        gradient_rows,
        preferred_element_type=jnp.float32,
    )
    probability_gradient = jnp.einsum(
        "ryk,oyk->yro", gradient_rows, value_matrix_rows, preferred_element_type=jnp.float32
    )
    score_gradient = (prob_full * (probability_gradient - correction_rows.T[:, :, None])).astype(
        jnp.bfloat16
    )
    d_query = (
        jnp.einsum(
            "tcg,gto->cto", score_gradient, key_matrix_rows, preferred_element_type=jnp.float32
        )
        * logit_scale
    )
    d_key = (
        jnp.einsum("jvy,vjk->yjk", score_gradient, query_matrix, preferred_element_type=jnp.float32)
        * logit_scale
    )
    return (d_query, d_key, value_gradient)


def local(signal, w_qkv, w_out, offsets, d_result):
    tok_rows = signal[0]
    upstream = d_result[0]
    t_dev, model_dim = tok_rows.shape
    head_total = HEADS
    head_dim = model_dim // head_total
    logit_scale = 1.0 / math.sqrt(head_dim)
    shards = lax.axis_size("seq")
    mid_rate = min(16, shards)
    mid_bits = mid_rate.bit_length() - 1
    shard_index = lax.axis_index("seq")
    mid_off = offsets[0]
    far_off = offsets[1]
    qkv_full, out_full = (
        lax.all_gather(w_qkv, "seq", axis=0, tiled=True),
        lax.all_gather(w_out, "seq", axis=0, tiled=True),
    )
    projected = jnp.dot(tok_rows, qkv_full, preferred_element_type=jnp.float32)
    qkv_rows = projected.astype(jnp.bfloat16)
    query_rows = qkv_rows[:, :model_dim].reshape(t_dev, head_total, head_dim)
    key_matrix_rows = qkv_rows[:, model_dim : 2 * model_dim].reshape(t_dev, head_total, head_dim)
    value_matrix_rows = qkv_rows[:, 2 * model_dim :].reshape(t_dev, head_total, head_dim)
    q_wide, q_factor = normalize(query_rows)
    k_wide, k_factor = normalize(key_matrix_rows)
    query_normalized = q_wide.astype(jnp.bfloat16)
    key_normalized = k_wide.astype(jnp.bfloat16)
    numer_near, denom_near = attend(
        query_normalized, key_normalized, value_matrix_rows, logit_scale
    )
    key_value = jnp.concatenate([key_normalized, value_matrix_rows], axis=2)
    mid_local = gather_row_subset(key_value, mid_rate, mid_off)
    far_local = gather_row_subset(key_value, shards, far_off)
    mid_all = mid_local
    for bit_num in range(mid_bits):
        partner = from_partner(mid_all, "seq", bit_num)
        mid_all = join_halves(mid_all, partner, shard_index // (1 << bit_num) % 2)
    far_all = lax.all_gather(far_local, "seq", axis=0, tiled=True)
    mid_keys_all = mid_all[..., :head_dim]
    mid_vals_all = mid_all[..., head_dim:]
    far_keys_all = far_all[..., :head_dim]
    far_vals_all = far_all[..., head_dim:]
    q_mid = gather_row_subset(query_normalized, mid_rate, mid_off)
    q_far = gather_row_subset(query_normalized, shards, far_off)
    numer_mid, denom_mid = attend(q_mid, mid_keys_all, mid_vals_all, logit_scale)
    numer_far, denom_far = attend(q_far, far_keys_all, far_vals_all, logit_scale)
    softmax_numerator = (
        numer_near
        + scatter_row_subset(numer_mid, mid_rate, mid_off)
        + scatter_row_subset(numer_far, shards, far_off)
    )
    softmax_denominator = (
        denom_near
        + scatter_row_subset(denom_mid[..., None], mid_rate, mid_off)[..., 0]
        + scatter_row_subset(denom_far[..., None], shards, far_off)[..., 0]
    )
    attn_three = (softmax_numerator / softmax_denominator[..., None]).astype(jnp.bfloat16)
    attn_rows = attn_three.reshape(t_dev, model_dim)
    layer_out = jnp.dot(attn_rows, out_full, preferred_element_type=jnp.float32)
    d_attn_wide = jnp.dot(upstream, out_full.T, preferred_element_type=jnp.float32)
    result = layer_out.astype(jnp.bfloat16)
    attention_gradient = d_attn_wide.astype(jnp.bfloat16).reshape(t_dev, head_total, head_dim)
    correction_rows = jnp.sum(
        attention_gradient.astype(jnp.float32) * attn_three.astype(jnp.float32), axis=-1
    )
    dq_near, dk_near, dv_near = attend_back(
        query_normalized,
        key_normalized,
        value_matrix_rows,
        attention_gradient,
        correction_rows,
        softmax_denominator,
        logit_scale,
    )
    g_mid = gather_row_subset(attention_gradient, mid_rate, mid_off)
    g_far = gather_row_subset(attention_gradient, shards, far_off)
    delta_mid = gather_row_subset(correction_rows[..., None], mid_rate, mid_off)[..., 0]
    delta_far = gather_row_subset(correction_rows[..., None], shards, far_off)[..., 0]
    denom_mid_q = gather_row_subset(softmax_denominator[..., None], mid_rate, mid_off)[..., 0]
    denom_far_q = gather_row_subset(softmax_denominator[..., None], shards, far_off)[..., 0]
    dq_mid, dk_mid_part, dv_mid_part = attend_back(
        q_mid, mid_keys_all, mid_vals_all, g_mid, delta_mid, denom_mid_q, logit_scale
    )
    dq_far, dk_far_part, dv_far_part = attend_back(
        q_far, far_keys_all, far_vals_all, g_far, delta_far, denom_far_q, logit_scale
    )
    query_pack = jnp.concatenate([q_mid, g_mid], axis=2)
    stat_pack = jnp.stack([delta_mid, denom_mid_q], axis=2)
    for bit_num in range(mid_bits):
        upper_bit = shard_index // (1 << bit_num) % 2
        peer_query = from_partner(query_pack, "seq", bit_num)
        peer_stats = from_partner(stat_pack, "seq", bit_num)
        query_pack = join_halves(query_pack, peer_query, upper_bit)
        stat_pack = join_halves(stat_pack, peer_stats, upper_bit)
    unused_mid, dk_mid, dv_mid = attend_back(
        query_pack[..., :head_dim],
        mid_local[..., :head_dim],
        mid_local[..., head_dim:],
        query_pack[..., head_dim:],
        stat_pack[..., 0],
        stat_pack[..., 1],
        logit_scale,
    )
    far_query_pack = lax.all_gather(
        jnp.concatenate([q_far, g_far], axis=2), "seq", axis=0, tiled=True
    )
    far_stat_pack = lax.all_gather(
        jnp.stack([delta_far, denom_far_q], axis=2), "seq", axis=0, tiled=True
    )
    unused_far, dk_far, dv_far = attend_back(
        far_query_pack[..., :head_dim],
        far_local[..., :head_dim],
        far_local[..., head_dim:],
        far_query_pack[..., head_dim:],
        far_stat_pack[..., 0],
        far_stat_pack[..., 1],
        logit_scale,
    )
    normed_query_gradient = (
        dq_near
        + scatter_row_subset(dq_mid, mid_rate, mid_off)
        + scatter_row_subset(dq_far, shards, far_off)
    )
    normed_key_gradient = (
        dk_near
        + scatter_row_subset(dk_mid, mid_rate, mid_off)
        + scatter_row_subset(dk_far, shards, far_off)
    )
    value_gradient = (
        dv_near
        + scatter_row_subset(dv_mid, mid_rate, mid_off)
        + scatter_row_subset(dv_far, shards, far_off)
    )
    d_query = q_factor * (
        normed_query_gradient
        - q_wide * jnp.mean(normed_query_gradient * q_wide, axis=-1, keepdims=True)
    )
    d_key = k_factor * (
        normed_key_gradient
        - k_wide * jnp.mean(normed_key_gradient * k_wide, axis=-1, keepdims=True)
    )
    d_qkv = jnp.concatenate(
        [
            d_query.reshape(t_dev, model_dim),
            d_key.reshape(t_dev, model_dim),
            value_gradient.reshape(t_dev, model_dim),
        ],
        axis=1,
    ).astype(jnp.bfloat16)
    d_input = jnp.dot(d_qkv, qkv_full.T, preferred_element_type=jnp.float32)
    d_signal = d_input.astype(jnp.bfloat16)
    grad_in = jnp.einsum("ti,tj->ij", tok_rows, d_qkv, preferred_element_type=jnp.float32)
    grad_mix = jnp.einsum("ti,tj->ij", attn_rows, upstream, preferred_element_type=jnp.float32)
    owned = lax.psum_scatter(
        jnp.concatenate([grad_in, grad_mix], axis=1), "seq", scatter_dimension=0, tiled=True
    )
    owned = lax.psum(owned, "rep")
    return (result[None], d_signal[None], owned[:, : 3 * model_dim], owned[:, 3 * model_dim :])


BF = jnp.bfloat16
F32 = jnp.float32
TD = 128
HD = 64
DM = 512
NN = (((1,), (0,)), ((), ()))
NT = (((1,), (1,)), ((), ()))
TN = (((0,), (0,)), ((), ()))


def mm(a, b, dims=NN):
    return lax.dot_general(a, b, dims, preferred_element_type=F32)


def low_lanes(rows):
    return lax.broadcasted_iota(jnp.int32, (rows, 128), 1) < HD


def swap_halves(tile):
    return pltpu.roll(tile.astype(F32), HD, 1)


def half_ones():
    a = lax.broadcasted_iota(jnp.int32, (128, 128), 0) < HD
    b = lax.broadcasted_iota(jnp.int32, (128, 128), 1) < HD
    return (a == b).astype(BF)


def half_means(values, ones):
    head = values.astype(BF)
    tail = (values - head.astype(F32)).astype(BF)
    return (mm(head, ones) + mm(tail, ones)) * (1.0 / HD)


W_AT = 4 * TD
D_AT = W_AT + 3 * HD
PAY = D_AT + 4 * TD


def pack_kernel(sig_ref, grad_ref, wqkv_ref, pay0, pay1, pay2, pay3, s_scr, d_scr, w_scr, sems):
    chip = lax.axis_index("seq") // 2
    low = low_lanes(HD)
    loads = [
        pltpu.make_async_copy(src, dst, sems.at[n])
        for n, (src, dst) in enumerate(((wqkv_ref, w_scr), (sig_ref, s_scr), (grad_ref, d_scr)))
    ]
    for load in loads:
        load.start()
    loads[0].wait()
    pays = (pay0, pay1, pay2, pay3)
    for t, pay in enumerate(pays):
        col = (chip ^ t) * 128
        q = w_scr[:, pl.ds(pl.multiple_of(col, 128), 128)].astype(F32)
        k = w_scr[:, pl.ds(pl.multiple_of(DM + col, 128), 128)].astype(F32)
        pay[W_AT : W_AT + HD, :] = jnp.where(low, q, swap_halves(k)).astype(BF)
        pay[W_AT + HD : W_AT + 2 * HD, :] = jnp.where(low, swap_halves(q), k).astype(BF)
        pay[W_AT + 2 * HD : D_AT, :] = w_scr[:, pl.ds(pl.multiple_of(2 * DM + col, 128), 128)]
    loads[1].wait()
    for pay in pays:
        for n in range(4):
            pay[TD * n : TD * n + TD, :] = s_scr[:, 128 * n : 128 * n + 128]
    loads[2].wait()
    for pay in pays:
        for n in range(4):
            pay[D_AT + TD * n : D_AT + TD * n + TD, :] = d_scr[:, 128 * n : 128 * n + 128]


def row_tiles(pay, at):
    return jnp.concatenate([pay[at + TD * n : at + TD * n + TD, :] for n in range(4)], axis=1)


def head_kernel(reps, off_ref, *refs):
    S, wo_ref = refs[0:8], refs[8]
    keep_ref, give_ref, w_ref, own_ref, chunks = *refs[9:13], refs[13 : 12 + reps]
    qk_scr, v_scr, acc_scr, qkw_scr, rho_scr, e_scr = refs[12 + reps : 18 + reps]
    g_scr, dqk_scr, dv_scr, dw_scr, dwo_scr = refs[18 + reps :]
    me = lax.axis_index("seq")
    chip, core, rep = me // 2, me % 2, lax.axis_index("rep")
    scale = 1.0 / math.sqrt(HD)
    low = low_lanes(TD)
    ones = half_ones()
    for m in range(8):
        rows = pl.ds(pl.multiple_of((me ^ m) * HD, HD), HD)
        w_ref[rows, 0:128] = S[m][pl.ds(pl.multiple_of(W_AT + core * HD, HD), HD), :]
        w_ref[rows, 128:256] = S[m][W_AT + 2 * HD : D_AT, :]
        w_ref[rows, 256:384] = S[m][pl.ds(pl.multiple_of(W_AT + (1 - core) * HD, HD), HD), :]

    def forward(qkn, vv):
        flipped = swap_halves(qkn)
        qn, kn = qkn[:, :HD].astype(BF), flipped[:, :HD].astype(BF)
        e = jnp.exp(mm(qn, kn, NT) * scale)
        den = jnp.sum(e, axis=1, keepdims=True)
        return e, jnp.where(low, mm(e.astype(BF), vv.astype(BF)), den)

    def backward(e, qkn, vv, grads, den):
        flipped = swap_halves(qkn)
        kz = jnp.where(low, flipped, 0.0).astype(BF)
        qz = jnp.where(low, 0.0, flipped).astype(BF)
        da = jnp.where(low, grads, 0.0).astype(BF)
        delta = grads[:, HD : HD + 1]
        prob = e * (1.0 / den)
        dv = mm(prob.astype(BF), da, TN)
        dp = mm(da, vv.astype(BF), NT)
        ds = (prob * (dp - delta)).astype(BF)
        return mm(ds, kz) + mm(ds, qz, TN), dv

    for m in range(8):
        rows = slice(TD * m, TD * m + TD)
        qkv = mm(row_tiles(S[m], 0), w_ref[:, 0:256]).astype(BF).astype(F32)
        qk = qkv[:, 0:128]
        pair = qkv[:, 128:256]
        vv = jnp.where(core == 1, swap_halves(pair), pair)
        rho = lax.rsqrt(half_means(qk * qk, ones) + 1e-6)
        qkw = qk * rho
        qkn = qkw.astype(BF).astype(F32)
        qkw_scr[rows, :] = qkw
        rho_scr[rows, :] = rho
        qk_scr[rows, :] = qkn
        v_scr[rows, :] = vv
        e, val = forward(qkn, vv)
        e_scr[rows, :] = e
        acc_scr[rows, :] = val
    picks = [pl.ds(off_ref[level, me], TD, stride=8) for level in range(2)]
    for level, pick in enumerate(picks):
        e, val = forward(qk_scr[pick, :], v_scr[pick, :])
        e_scr[1024 + TD * level : 1024 + TD * level + TD, :] = e
        acc_scr[pick, :] = acc_scr[pick, :] + val

    wide = jnp.concatenate([wo_ref[...], jnp.zeros((HD, DM), BF)], axis=0)
    for m in range(8):
        rows = slice(TD * m, TD * m + TD)
        acc = acc_scr[rows, :]
        attn = jnp.where(low, acc / swap_halves(acc), 0.0).astype(BF)
        upstream = row_tiles(S[m], D_AT)
        da = mm(upstream, wide, NT).astype(BF).astype(F32)
        delta = jnp.sum(da * attn.astype(F32), axis=1, keepdims=True)
        grads = jnp.where(low, da, delta)
        g_scr[rows, :] = grads
        part = mm(attn, upstream, TN)
        dwo = part if m == 0 else dwo + part
        dqk, dv = backward(
            e_scr[rows, :], qk_scr[rows, :], v_scr[rows, :], grads, acc[:, HD : HD + 1]
        )
        dqk_scr[rows, :] = dqk
        dv_scr[rows, :] = jnp.where(low, dv, swap_halves(attn))
    dwo_scr[...] = dwo[:HD, :]
    for level, pick in enumerate(picks):
        dqk, dv = backward(
            e_scr[1024 + TD * level : 1024 + TD * level + TD, :],
            qk_scr[pick, :],
            v_scr[pick, :],
            g_scr[pick, :],
            acc_scr[pick, :][:, HD : HD + 1],
        )
        dqk_scr[pick, :] = dqk_scr[pick, :] + dqk
        dv_scr[pick, :] = dv_scr[pick, :] + jnp.where(low, dv, 0.0)
    for m in range(8):
        rows = slice(TD * m, TD * m + TD)
        dqk = dqk_scr[rows, :] * scale
        qkw = qkw_scr[rows, :]
        dqk = rho_scr[rows, :] * (dqk - qkw * half_means(dqk * qkw, ones))
        tile = jnp.concatenate([dqk.astype(BF), dv_scr[rows, :].astype(BF)], axis=1)
        ref = give_ref if m % 2 else keep_ref
        ref[TD * (m // 2) : TD * (m // 2) + TD, :] = tile
        part = mm(row_tiles(S[m], 0), tile, TN)
        if m == 0:
            dw_scr[...] = part
        else:
            dw_scr[...] = dw_scr[...] + part
    half = low_lanes(HD)

    def chunk(j):
        at = pl.multiple_of(((chip ^ rep ^ j) % 4) * TD, TD)
        first, second = dw_scr[pl.ds(at, HD), :], dw_scr[pl.ds(at + HD, HD), :]
        dv = jnp.where(half, first[:, 128:256], pltpu.roll(second[:, 128:256], HD, 1))
        return first[:, 0:128], second[:, 0:128], dv, dwo_scr[:, pl.ds(at, 128)]

    for j in range(reps):
        ref = chunks[j - 1] if j else own_ref
        for n, value in enumerate(chunk(j)):
            ref[HD * n : HD * n + HD, :] = value.astype(ref.dtype)


def project_kernel(keep_ref, got_ref, w_ref, wo_ref, wo_mate_ref, *outs):
    core = lax.axis_index("seq") % 2
    low = low_lanes(TD)
    wo = jnp.concatenate([wo_ref[...], wo_mate_ref[...]], axis=0)
    for t, out in enumerate(outs):
        rows = slice(TD * t, TD * t + TD)
        a, b = keep_ref[rows, 128:256].astype(F32), got_ref[rows, 128:256].astype(F32)
        attn = jnp.where(low, pltpu.roll(a, HD, 1), b).astype(BF)
        even, odd = jnp.where(core == 1, b, a), jnp.where(core == 1, a, b)
        dv = jnp.where(low, even, pltpu.roll(odd, HD, 1)).astype(BF)
        d_all = jnp.concatenate([keep_ref[rows, 0:128], dv, got_ref[rows, 0:128]], axis=1)
        out[:, 0:DM] = mm(attn, wo).astype(out.dtype)
        out[:, DM:] = mm(d_all, w_ref[...], NT).astype(out.dtype)


def add_kernel(*refs):
    total = refs[0][...].astype(F32)
    for ref in refs[1:-2]:
        total = total + ref[...].astype(F32)
    refs[-2][...] = total[:, 0:DM].astype(BF)
    refs[-1][...] = total[:, DM:].astype(BF)


def sum_kernel(*refs):
    total = refs[0][...]
    for ref in refs[1:-2]:
        total = total + ref[...].astype(F32)
    refs[-2][...] = total[0 : 3 * HD, :].astype(BF)
    refs[-1][...] = total[3 * HD :, :].astype(BF)


def total_kernel(*refs):
    F, (dw_ref, dwo_ref) = refs[:-2], refs[-2:]
    me = lax.axis_index("seq")
    chip, core = me // 2, me % 2
    rep = lax.axis_index("rep")
    low = low_lanes(HD)
    mine = pl.ds(pl.multiple_of(core * HD, HD), HD)
    for j in range(4):
        col = ((chip ^ rep ^ j) % 4) * 128
        a, b = F[2 * j], F[2 * j + 1]
        aqk, bqk = a[mine, :].astype(F32), b[mine, :].astype(F32)
        av, bv = a[TD : 3 * HD, :].astype(F32), b[TD : 3 * HD, :].astype(F32)
        even, odd = jnp.where(core == 1, bqk, aqk), jnp.where(core == 1, aqk, bqk)
        v = jnp.where(
            low,
            jnp.where(core == 1, pltpu.roll(bv, HD, 1), av),
            jnp.where(core == 1, av, pltpu.roll(bv, HD, 1)),
        )
        tiles = (
            jnp.where(low, even, pltpu.roll(odd, HD, 1)),
            jnp.where(low, pltpu.roll(even, HD, 1), odd),
            v,
        )
        for part, tile in enumerate(tiles):
            dw_ref[:, pl.ds(pl.multiple_of(part * DM + col, 128), 128)] = tile
        dwo_ref[:, pl.ds(pl.multiple_of(col, 128), 128)] = a[3 * HD :, :].astype(F32)


def vmem_call(body, ins, outs, scratch=(), flops=0, smem=0, raw=0):
    bytes_moved = sum(x.size * x.dtype.itemsize for x in list(ins) + list(outs))
    vmem = pl.BlockSpec(memory_space=pltpu.VMEM)
    specs = [pl.BlockSpec(memory_space=pltpu.SMEM)] * smem + [pl.BlockSpec(memory_space=pltpu.HBM)] * raw
    return pl.pallas_call(
        body,
        out_shape=list(outs),
        in_specs=specs + [vmem] * (len(ins) - smem - raw),
        out_specs=[vmem] * len(outs),
        scratch_shapes=list(scratch),
        compiler_params=pltpu.CompilerParams(vmem_limit_bytes=24 << 20),
        cost_estimate=pl.CostEstimate(flops=flops, bytes_accessed=bytes_moved, transcendentals=0),
    )(*ins)


def swap(value, mask, axis):
    return lax.ppermute(value, axis, [(i, i ^ mask) for i in range(lax.axis_size(axis))])


def shape(rows, cols, dtype=BF):
    return jax.ShapeDtypeStruct((rows, cols), dtype)


def after(value, *others):
    return lax.optimization_barrier((value, *others))[0]


def spread(parts, gates=(None,) * 4):
    out = [None] * 8
    for t in range(4):
        part = parts[t] if gates[t] is None else after(parts[t], gates[t])
        out[2 * t] = part if t == 0 else swap(part, 2 * t, "seq")
    for t in range(4):
        out[2 * t + 1] = swap(out[2 * t], 1, "seq")
    return out


def to_owner_chip(value):
    reps, seq = lax.axis_size("rep"), lax.axis_size("seq")
    pairs = [
        ((2 * a + c) * reps + r, (2 * ((a ^ r) % 4) + c) * reps + r)
        for r in range(reps)
        for a in range(seq // 2)
        for c in range(2)
    ]
    return lax.ppermute(value, ("seq", "rep"), pairs)


def local_heads(signal, w_qkv, w_out, offsets, d_result):
    sig, grad = signal[0], d_result[0]
    reps = lax.axis_size("rep")
    pays = vmem_call(
        pack_kernel,
        [pltpu.with_memory_space_constraint(x, pltpu.HBM) for x in (sig, grad, w_qkv)],
        [shape(PAY, 128)] * 4,
        scratch=[
            pltpu.VMEM((TD, DM), BF),
            pltpu.VMEM((TD, DM), BF),
            pltpu.VMEM((HD, 3 * DM), BF),
            pltpu.SemaphoreType.DMA((3,)),
        ],
        raw=3,
    )
    S = spread(pays)
    scr = [pltpu.VMEM((1024, 128), F32)]
    res = vmem_call(
        functools.partial(head_kernel, reps),
        (offsets, *S, w_out),
        [shape(4 * TD, 256)] * 2
        + [shape(DM, 384), shape(2 * TD, 128, F32)]
        + [shape(2 * TD, 128)] * (reps - 1),
        scratch=scr * 5
        + [pltpu.VMEM((1280, 128), F32)]
        + scr * 3
        + [pltpu.VMEM((DM, 256), F32), pltpu.VMEM((HD, DM), F32)],
        flops=10**9,
        smem=1,
    )
    keep, give, w_both, own, *chunks = res
    arrived = [swap(chunks[j - 1], j, "rep") for j in range(1, reps)]
    Y = vmem_call(
        project_kernel,
        (keep, swap(give, 1, "seq"), w_both, w_out, swap(w_out, 1, "seq")),
        [shape(TD, 2 * DM, F32)] + [shape(TD, 2 * DM)] * 3,
        flops=5 * 10**8,
    )
    own = after(own, *Y)
    total, dwo_part = vmem_call(
        sum_kernel, (own, *arrived), [shape(3 * HD, 128), shape(HD, 128)]
    )
    Y = [*Y[:3], after(Y[3], total)]
    Y = [Y[0]] + [swap(Y[t], 2 * t, "seq") for t in range(1, 4)]
    result, d_signal = vmem_call(add_kernel, Y, [shape(TD, DM)] * 2)
    rows = jnp.concatenate([to_owner_chip(total), dwo_part], axis=0)
    F = []
    for j in range(reps):
        same = swap(rows, j, "rep") if j else rows
        F += [same, swap(after(same, result) if j == reps - 1 else same, 1, "seq")]
    dw, dwo = vmem_call(
        total_kernel,
        F,
        [shape(HD, 3 * DM, F32), shape(HD, DM, F32)],
    )
    return (result[None], d_signal[None], dw, dwo)


def solution(mesh):
    in_specs = (P("rep", "seq", None), P("seq", None), P("seq", None), P(), P("rep", "seq", None))
    out_specs = (P("rep", "seq", None), P("rep", "seq", None), P("seq", None), P("seq", None))

    def body(signal, w_qkv, w_out, offsets, d_result):
        reps = mesh.shape["rep"]
        per_head = mesh.shape["seq"] == HEADS and reps == 4
        if per_head and signal.shape == (1, TD, DM) and w_qkv.shape == (HD, 3 * DM):
            return local_heads(signal, w_qkv, w_out, offsets, d_result)
        return local(signal, w_qkv, w_out, offsets, d_result)

    return jax.shard_map(body, mesh=mesh, in_specs=in_specs, out_specs=out_specs, check_vma=False)
```

```python
import functools
import math

import jax
import jax.numpy as jnp
from jax import lax
from jax.experimental import pallas as pl
from jax.experimental.pallas import tpu as pltpu
from jax.sharding import PartitionSpec as P

HEADS = 8


def from_partner(value, axis, stride):
    mask = 2**stride
    pairs = [(source, source ^ mask) for source in range(lax.axis_size(axis))]
    return lax.ppermute(value, axis, pairs)


def normalize(tensor):
    widened = tensor.astype(jnp.float32)
    factor = lax.rsqrt(jnp.mean(widened * widened, axis=-1, keepdims=True) + 1e-06)
    return (widened * factor, factor)


def gather_row_subset(full_row_tensor, dilation_step, start_shift):
    row_total = full_row_tensor.shape[0] // dilation_step
    reshaped_tensor = full_row_tensor.reshape(
        row_total, dilation_step, full_row_tensor.shape[1], full_row_tensor.shape[2]
    )
    chosen_rows_list = jnp.arange(dilation_step)[:, None] == start_shift[None, :]
    kept_rows = jnp.where(
        chosen_rows_list[None, :, :, None], reshaped_tensor, jnp.zeros((), full_row_tensor.dtype)
    )
    return jnp.sum(kept_rows, axis=1)


def scatter_row_subset(gathered_rows, dilation_step, start_shift):
    row_total, head_total, feature_count = gathered_rows.shape
    chosen_rows_list = jnp.arange(dilation_step)[:, None] == start_shift[None, :]
    scattered_rows = jnp.where(
        chosen_rows_list[None, :, :, None],
        gathered_rows[:, None],
        jnp.zeros((), gathered_rows.dtype),
    )
    return scattered_rows.reshape(row_total * dilation_step, head_total, feature_count)


def join_halves(own_part, peer_part, upper_bit):
    return jnp.where(
        upper_bit == 1,
        jnp.concatenate([peer_part, own_part], axis=0),
        jnp.concatenate([own_part, peer_part], axis=0),
    )


def attend(query_matrix, key_matrix_rows, value_matrix_rows, logit_scale):
    scores = (
        jnp.einsum(
            "ryk,oyk->yro", query_matrix, key_matrix_rows, preferred_element_type=jnp.float32
        )
        * logit_scale
    )
    exp_scores = jnp.exp(scores)
    softmax_denominator = jnp.sum(exp_scores, axis=-1).T
    softmax_numerator = jnp.einsum(
        "tcg,gto->cto",
        exp_scores.astype(jnp.bfloat16),
        value_matrix_rows,
        preferred_element_type=jnp.float32,
    )
    return (softmax_numerator, softmax_denominator)


def attend_back(
    query_matrix,
    key_matrix_rows,
    value_matrix_rows,
    gradient_rows,
    correction_rows,
    denom_rows,
    logit_scale,
):
    scores = (
        jnp.einsum(
            "ryk,oyk->yro", query_matrix, key_matrix_rows, preferred_element_type=jnp.float32
        )
        * logit_scale
    )
    prob_full = jnp.exp(scores) / denom_rows.T[:, :, None]
    value_gradient = jnp.einsum(
        "jvy,vjk->yjk",
        prob_full.astype(jnp.bfloat16),
        gradient_rows,
        preferred_element_type=jnp.float32,
    )
    probability_gradient = jnp.einsum(
        "ryk,oyk->yro", gradient_rows, value_matrix_rows, preferred_element_type=jnp.float32
    )
    score_gradient = (prob_full * (probability_gradient - correction_rows.T[:, :, None])).astype(
        jnp.bfloat16
    )
    d_query = (
        jnp.einsum(
            "tcg,gto->cto", score_gradient, key_matrix_rows, preferred_element_type=jnp.float32
        )
        * logit_scale
    )
    d_key = (
        jnp.einsum("jvy,vjk->yjk", score_gradient, query_matrix, preferred_element_type=jnp.float32)
        * logit_scale
    )
    return (d_query, d_key, value_gradient)


def local(signal, w_qkv, w_out, offsets, d_result):
    tok_rows = signal[0]
    upstream = d_result[0]
    t_dev, model_dim = tok_rows.shape
    head_total = HEADS
    head_dim = model_dim // head_total
    logit_scale = 1.0 / math.sqrt(head_dim)
    shards = lax.axis_size("seq")
    mid_rate = min(16, shards)
    mid_bits = mid_rate.bit_length() - 1
    shard_index = lax.axis_index("seq")
    mid_off = offsets[0]
    far_off = offsets[1]
    qkv_full, out_full = (
        lax.all_gather(w_qkv, "seq", axis=0, tiled=True),
        lax.all_gather(w_out, "seq", axis=0, tiled=True),
    )
    projected = jnp.dot(tok_rows, qkv_full, preferred_element_type=jnp.float32)
    qkv_rows = projected.astype(jnp.bfloat16)
    query_rows = qkv_rows[:, :model_dim].reshape(t_dev, head_total, head_dim)
    key_matrix_rows = qkv_rows[:, model_dim : 2 * model_dim].reshape(t_dev, head_total, head_dim)
    value_matrix_rows = qkv_rows[:, 2 * model_dim :].reshape(t_dev, head_total, head_dim)
    q_wide, q_factor = normalize(query_rows)
    k_wide, k_factor = normalize(key_matrix_rows)
    query_normalized = q_wide.astype(jnp.bfloat16)
    key_normalized = k_wide.astype(jnp.bfloat16)
    numer_near, denom_near = attend(
        query_normalized, key_normalized, value_matrix_rows, logit_scale
    )
    key_value = jnp.concatenate([key_normalized, value_matrix_rows], axis=2)
    mid_local = gather_row_subset(key_value, mid_rate, mid_off)
    far_local = gather_row_subset(key_value, shards, far_off)
    mid_all = mid_local
    for bit_num in range(mid_bits):
        partner = from_partner(mid_all, "seq", bit_num)
        mid_all = join_halves(mid_all, partner, shard_index // (1 << bit_num) % 2)
    far_all = lax.all_gather(far_local, "seq", axis=0, tiled=True)
    mid_keys_all = mid_all[..., :head_dim]
    mid_vals_all = mid_all[..., head_dim:]
    far_keys_all = far_all[..., :head_dim]
    far_vals_all = far_all[..., head_dim:]
    q_mid = gather_row_subset(query_normalized, mid_rate, mid_off)
    q_far = gather_row_subset(query_normalized, shards, far_off)
    numer_mid, denom_mid = attend(q_mid, mid_keys_all, mid_vals_all, logit_scale)
    numer_far, denom_far = attend(q_far, far_keys_all, far_vals_all, logit_scale)
    softmax_numerator = (
        numer_near
        + scatter_row_subset(numer_mid, mid_rate, mid_off)
        + scatter_row_subset(numer_far, shards, far_off)
    )
    softmax_denominator = (
        denom_near
        + scatter_row_subset(denom_mid[..., None], mid_rate, mid_off)[..., 0]
        + scatter_row_subset(denom_far[..., None], shards, far_off)[..., 0]
    )
    attn_three = (softmax_numerator / softmax_denominator[..., None]).astype(jnp.bfloat16)
    attn_rows = attn_three.reshape(t_dev, model_dim)
    layer_out = jnp.dot(attn_rows, out_full, preferred_element_type=jnp.float32)
    d_attn_wide = jnp.dot(upstream, out_full.T, preferred_element_type=jnp.float32)
    result = layer_out.astype(jnp.bfloat16)
    attention_gradient = d_attn_wide.astype(jnp.bfloat16).reshape(t_dev, head_total, head_dim)
    correction_rows = jnp.sum(
        attention_gradient.astype(jnp.float32) * attn_three.astype(jnp.float32), axis=-1
    )
    dq_near, dk_near, dv_near = attend_back(
        query_normalized,
        key_normalized,
        value_matrix_rows,
        attention_gradient,
        correction_rows,
        softmax_denominator,
        logit_scale,
    )
    g_mid = gather_row_subset(attention_gradient, mid_rate, mid_off)
    g_far = gather_row_subset(attention_gradient, shards, far_off)
    delta_mid = gather_row_subset(correction_rows[..., None], mid_rate, mid_off)[..., 0]
    delta_far = gather_row_subset(correction_rows[..., None], shards, far_off)[..., 0]
    denom_mid_q = gather_row_subset(softmax_denominator[..., None], mid_rate, mid_off)[..., 0]
    denom_far_q = gather_row_subset(softmax_denominator[..., None], shards, far_off)[..., 0]
    dq_mid, dk_mid_part, dv_mid_part = attend_back(
        q_mid, mid_keys_all, mid_vals_all, g_mid, delta_mid, denom_mid_q, logit_scale
    )
    dq_far, dk_far_part, dv_far_part = attend_back(
        q_far, far_keys_all, far_vals_all, g_far, delta_far, denom_far_q, logit_scale
    )
    query_pack = jnp.concatenate([q_mid, g_mid], axis=2)
    stat_pack = jnp.stack([delta_mid, denom_mid_q], axis=2)
    for bit_num in range(mid_bits):
        upper_bit = shard_index // (1 << bit_num) % 2
        peer_query = from_partner(query_pack, "seq", bit_num)
        peer_stats = from_partner(stat_pack, "seq", bit_num)
        query_pack = join_halves(query_pack, peer_query, upper_bit)
        stat_pack = join_halves(stat_pack, peer_stats, upper_bit)
    unused_mid, dk_mid, dv_mid = attend_back(
        query_pack[..., :head_dim],
        mid_local[..., :head_dim],
        mid_local[..., head_dim:],
        query_pack[..., head_dim:],
        stat_pack[..., 0],
        stat_pack[..., 1],
        logit_scale,
    )
    far_query_pack = lax.all_gather(
        jnp.concatenate([q_far, g_far], axis=2), "seq", axis=0, tiled=True
    )
    far_stat_pack = lax.all_gather(
        jnp.stack([delta_far, denom_far_q], axis=2), "seq", axis=0, tiled=True
    )
    unused_far, dk_far, dv_far = attend_back(
        far_query_pack[..., :head_dim],
        far_local[..., :head_dim],
        far_local[..., head_dim:],
        far_query_pack[..., head_dim:],
        far_stat_pack[..., 0],
        far_stat_pack[..., 1],
        logit_scale,
    )
    normed_query_gradient = (
        dq_near
        + scatter_row_subset(dq_mid, mid_rate, mid_off)
        + scatter_row_subset(dq_far, shards, far_off)
    )
    normed_key_gradient = (
        dk_near
        + scatter_row_subset(dk_mid, mid_rate, mid_off)
        + scatter_row_subset(dk_far, shards, far_off)
    )
    value_gradient = (
        dv_near
        + scatter_row_subset(dv_mid, mid_rate, mid_off)
        + scatter_row_subset(dv_far, shards, far_off)
    )
    d_query = q_factor * (
        normed_query_gradient
        - q_wide * jnp.mean(normed_query_gradient * q_wide, axis=-1, keepdims=True)
    )
    d_key = k_factor * (
        normed_key_gradient
        - k_wide * jnp.mean(normed_key_gradient * k_wide, axis=-1, keepdims=True)
    )
    d_qkv = jnp.concatenate(
        [
            d_query.reshape(t_dev, model_dim),
            d_key.reshape(t_dev, model_dim),
            value_gradient.reshape(t_dev, model_dim),
        ],
        axis=1,
    ).astype(jnp.bfloat16)
    d_input = jnp.dot(d_qkv, qkv_full.T, preferred_element_type=jnp.float32)
    d_signal = d_input.astype(jnp.bfloat16)
    grad_in = jnp.einsum("ti,tj->ij", tok_rows, d_qkv, preferred_element_type=jnp.float32)
    grad_mix = jnp.einsum("ti,tj->ij", attn_rows, upstream, preferred_element_type=jnp.float32)
    owned = lax.psum_scatter(
        jnp.concatenate([grad_in, grad_mix], axis=1), "seq", scatter_dimension=0, tiled=True
    )
    owned = lax.psum(owned, "rep")
    return (result[None], d_signal[None], owned[:, : 3 * model_dim], owned[:, 3 * model_dim :])


BF = jnp.bfloat16
F32 = jnp.float32
TD = 128
HD = 64
DM = 512
NN = (((1,), (0,)), ((), ()))
NT = (((1,), (1,)), ((), ()))
TN = (((0,), (0,)), ((), ()))


def mm(a, b, dims=NN):
    return lax.dot_general(a, b, dims, preferred_element_type=F32)


def low_lanes(rows):
    return lax.broadcasted_iota(jnp.int32, (rows, 128), 1) < HD


def swap_halves(tile):
    return pltpu.roll(tile.astype(F32), HD, 1)


W_AT = 4 * TD
D_AT = W_AT + 3 * HD
PAY = D_AT + 4 * TD


def pack_kernel(sig_ref, grad_ref, wqkv_ref, pay0, pay1, pay2, pay3, s_scr, d_scr, w_scr, sems):
    chip = lax.axis_index("seq") // 2
    low = low_lanes(HD)
    loads = [
        pltpu.make_async_copy(src, dst, sems.at[n])
        for n, (src, dst) in enumerate(((wqkv_ref, w_scr), (sig_ref, s_scr), (grad_ref, d_scr)))
    ]
    for load in loads:
        load.start()
    loads[0].wait()
    pays = (pay0, pay1, pay2, pay3)
    for t, pay in enumerate(pays):
        col = (chip ^ t) * 128
        q = w_scr[:, pl.ds(pl.multiple_of(col, 128), 128)].astype(F32)
        k = w_scr[:, pl.ds(pl.multiple_of(DM + col, 128), 128)].astype(F32)
        pay[W_AT : W_AT + HD, :] = jnp.where(low, q, swap_halves(k)).astype(BF)
        pay[W_AT + HD : W_AT + 2 * HD, :] = jnp.where(low, swap_halves(q), k).astype(BF)
        pay[W_AT + 2 * HD : D_AT, :] = w_scr[:, pl.ds(pl.multiple_of(2 * DM + col, 128), 128)]
    loads[1].wait()
    for pay in pays:
        for n in range(4):
            pay[TD * n : TD * n + TD, :] = s_scr[:, 128 * n : 128 * n + 128]
    loads[2].wait()
    for pay in pays:
        for n in range(4):
            pay[D_AT + TD * n : D_AT + TD * n + TD, :] = d_scr[:, 128 * n : 128 * n + 128]


def row_tiles(pay, at):
    return jnp.concatenate([pay[at + TD * n : at + TD * n + TD, :] for n in range(4)], axis=1)


def stack(parts):
    return jnp.concatenate(parts, axis=0)


def halves(values):
    head = values.astype(BF)
    return jnp.concatenate([head, (values - head.astype(F32)).astype(BF)], axis=1)


def lanes_where(rows, test):
    a = lax.broadcasted_iota(jnp.int32, (rows, 128), 0) % 128
    b = lax.broadcasted_iota(jnp.int32, (rows, 128), 1)
    return test(a, b).astype(F32).astype(BF)


def head_kernel(reps, off_ref, *refs):
    S, wo_ref = refs[0:8], refs[8]
    keep_ref, give_ref, w_ref, own_ref, chunks = *refs[9:13], refs[13 : 12 + reps]
    qk_scr, v_scr, acc_scr, g_scr, dq_scr, dvk_scr, dw_scr = refs[12 + reps :]
    me = lax.axis_index("seq")
    chip, core, rep = me // 2, me % 2, lax.axis_index("rep")
    scale = 1.0 / math.sqrt(HD)
    low = low_lanes(TD)
    same_half = lanes_where(256, lambda a, b: (a < HD) == (b < HD))
    low_to_high = lanes_where(256, lambda a, b: (a < HD) & (b >= HD))
    ones_high = lanes_where(TD, lambda a, b: b >= HD)
    blocks = [slice(TD * m, TD * m + TD) for m in range(8)]
    picks = [pl.ds(off_ref[level, me], TD, stride=8) for level in range(2)]

    def spread_high(tile):
        return jnp.where(low, swap_halves(tile), tile)

    for m in range(8):
        rows = pl.ds(pl.multiple_of((me ^ m) * HD, HD), HD)
        w_ref[rows, 0:128] = S[m][pl.ds(pl.multiple_of(W_AT + core * HD, HD), HD), :]
        w_ref[rows, 128:256] = S[m][W_AT + 2 * HD : D_AT, :]
        w_ref[rows, 256:384] = S[m][pl.ds(pl.multiple_of(W_AT + (1 - core) * HD, HD), HD), :]
    x = stack([row_tiles(S[m], 0) for m in range(8)])
    upstream = stack([row_tiles(S[m], D_AT) for m in range(8)])
    wide = stack([wo_ref[...], jnp.zeros((HD, DM), BF)])
    da = mm(upstream, wide, NT).astype(BF)
    qkv = mm(x, w_ref[:, 0:256]).astype(BF).astype(F32)
    qk, pair = qkv[:, 0:128], qkv[:, 128:256]
    vv = jnp.where(core == 1, swap_halves(pair), pair)
    rho = lax.rsqrt(mm(halves(qk * qk), same_half) * (1.0 / HD) + 1e-6)
    qkw = qk * rho
    qkn = qkw.astype(BF).astype(F32)
    qk_scr[...] = qkn
    v_scr[...] = vv
    flipped = swap_halves(qkn)

    def forward(qkn, flipped, vv):
        s = mm(qkn[:, :HD].astype(BF), flipped[:, :HD].astype(BF), NT)
        return jnp.exp(s * scale)

    def weigh(e, vv):
        right = stack([jnp.where(low, vv, 1.0).astype(BF), ones_high])
        return mm(halves(e), right)

    near = [forward(qkn[b], flipped[b], vv[b]) for b in blocks]
    for b, e in zip(blocks, near):
        acc_scr[b, :] = weigh(e, vv[b])
    far = [(qk_scr[pick, :], v_scr[pick, :]) for pick in picks]
    far = [(q, swap_halves(q), v) for q, v in far]
    far_e = [forward(*tiles) for tiles in far]
    for pick, e, (_, _, v) in zip(picks, far_e, far):
        acc_scr[pick, :] = acc_scr[pick, :] + weigh(e, v)

    accs = [acc_scr[b, :] for b in blocks]
    rdens = [1.0 / spread_high(acc) for acc in accs]
    attns = [jnp.where(low, acc * r, 0.0).astype(BF) for acc, r in zip(accs, rdens)]
    dot_terms = da.astype(F32) * stack(attns).astype(F32)
    grads = da.astype(F32) + mm(halves(dot_terms), low_to_high)
    g_scr[...] = grads

    def backward(e, rden, flipped, vv, da, delta):
        prob = e * rden
        dp = mm(da, vv.astype(BF), NT)
        ds = (prob * (dp - delta)).astype(BF)
        dq = mm(ds, flipped.astype(BF))
        qz = jnp.where(low, 0.0, flipped).astype(BF)
        return dq, mm(stack([prob.astype(BF), ds]), stack([da, qz]), TN)

    for m, b in enumerate(blocks):
        dq, dvk = backward(
            near[m], rdens[m], flipped[b], vv[b], da[b], spread_high(grads[b])
        )
        dq_scr[b, :] = dq
        dvk_scr[b, :] = dvk
    for pick, e, (_, f, v) in zip(picks, far_e, far):
        g = g_scr[pick, :]
        dq, dvk = backward(
            e,
            1.0 / spread_high(acc_scr[pick, :]),
            f,
            v,
            jnp.where(low, g, 0.0).astype(BF),
            spread_high(g),
        )
        dq_scr[pick, :] = dq_scr[pick, :] + dq
        dvk_scr[pick, :] = dvk_scr[pick, :] + dvk

    low_all = low_lanes(1024)
    dvk = dvk_scr[...]
    dqk = jnp.where(low_all, dq_scr[...], dvk) * scale
    mean = mm(halves(dqk * qkw), same_half) * (1.0 / HD)
    dqk = (rho * (dqk - qkw * mean)).astype(BF)
    attn_high = swap_halves(stack(attns))
    tile = jnp.concatenate([dqk, jnp.where(low_all, dvk, attn_high).astype(BF)], axis=1)
    for m, b in enumerate(blocks):
        ref = give_ref if m % 2 else keep_ref
        ref[TD * (m // 2) : TD * (m // 2) + TD, :] = tile[b]
    dw_scr[0 : 3 * HD, :] = mm(tile[:, 0 : 3 * HD], x, TN)
    dw_scr[3 * HD :, :] = mm(stack(attns), upstream, TN)[:HD]
    for j in range(reps):
        ref = chunks[j - 1] if j else own_ref
        at = pl.multiple_of(((chip ^ rep ^ j) % 4) * TD, TD)
        ref[...] = dw_scr[:, pl.ds(at, 128)].astype(ref.dtype)


def project_kernel(keep_ref, got_ref, w_ref, wo_ref, wo_mate_ref, *outs):
    core = lax.axis_index("seq") % 2
    low = low_lanes(TD)
    wo = jnp.concatenate([wo_ref[...], wo_mate_ref[...]], axis=0)
    for t, out in enumerate(outs):
        rows = slice(TD * t, TD * t + TD)
        a, b = keep_ref[rows, 128:256].astype(F32), got_ref[rows, 128:256].astype(F32)
        attn = jnp.where(low, pltpu.roll(a, HD, 1), b).astype(BF)
        even, odd = jnp.where(core == 1, b, a), jnp.where(core == 1, a, b)
        dv = jnp.where(low, even, pltpu.roll(odd, HD, 1)).astype(BF)
        d_all = jnp.concatenate([keep_ref[rows, 0:128], dv, got_ref[rows, 0:128]], axis=1)
        out[:, 0:DM] = mm(attn, wo).astype(out.dtype)
        out[:, DM:] = mm(d_all, w_ref[...], NT).astype(out.dtype)


def add_kernel(*refs):
    total = refs[0][...].astype(F32)
    for ref in refs[1:-2]:
        total = total + ref[...].astype(F32)
    refs[-2][...] = total[:, 0:DM].astype(BF)
    refs[-1][...] = total[:, DM:].astype(BF)


def sum_kernel(*refs):
    total = refs[0][...]
    for ref in refs[1:-2]:
        total = total + ref[...].astype(F32)
    dv = total[TD : 3 * HD]
    turned = stack([dv, dv]).T
    refs[-2][0:TD, :] = total[0:TD].T.astype(BF)
    refs[-2][TD:, :] = jnp.where(low_lanes(HD), turned[:HD], turned[HD:]).astype(BF)
    refs[-1][...] = total[3 * HD :].astype(BF)


def total_kernel(*refs):
    F, (dw_ref, dwo_ref) = refs[:-2], refs[-2:]
    me = lax.axis_index("seq")
    chip, core = me // 2, me % 2
    rep = lax.axis_index("rep")
    low = low_lanes(HD)
    mine = pl.ds(pl.multiple_of(core * HD, HD), HD)
    for j in range(4):
        col = ((chip ^ rep ^ j) % 4) * 128
        a, b = F[2 * j], F[2 * j + 1]
        aqk, bqk = a[mine, :].astype(F32), b[mine, :].astype(F32)
        av, bv = a[TD : 3 * HD, :].astype(F32), b[TD : 3 * HD, :].astype(F32)
        even, odd = jnp.where(core == 1, bqk, aqk), jnp.where(core == 1, aqk, bqk)
        v = jnp.where(
            low,
            jnp.where(core == 1, pltpu.roll(bv, HD, 1), av),
            jnp.where(core == 1, av, pltpu.roll(bv, HD, 1)),
        )
        tiles = (
            jnp.where(low, even, pltpu.roll(odd, HD, 1)),
            jnp.where(low, pltpu.roll(even, HD, 1), odd),
            v,
        )
        for part, tile in enumerate(tiles):
            dw_ref[:, pl.ds(pl.multiple_of(part * DM + col, 128), 128)] = tile
        dwo_ref[:, pl.ds(pl.multiple_of(col, 128), 128)] = a[3 * HD :, :].astype(F32)


def vmem_call(body, ins, outs, scratch=(), flops=0, smem=0, raw=0):
    bytes_moved = sum(x.size * x.dtype.itemsize for x in list(ins) + list(outs))
    vmem = pl.BlockSpec(memory_space=pltpu.VMEM)
    specs = [pl.BlockSpec(memory_space=pltpu.SMEM)] * smem + [pl.BlockSpec(memory_space=pltpu.HBM)] * raw
    return pl.pallas_call(
        body,
        out_shape=list(outs),
        in_specs=specs + [vmem] * (len(ins) - smem - raw),
        out_specs=[vmem] * len(outs),
        scratch_shapes=list(scratch),
        compiler_params=pltpu.CompilerParams(vmem_limit_bytes=24 << 20),
        cost_estimate=pl.CostEstimate(flops=flops, bytes_accessed=bytes_moved, transcendentals=0),
    )(*ins)


def swap(value, mask, axis):
    return lax.ppermute(value, axis, [(i, i ^ mask) for i in range(lax.axis_size(axis))])


def shape(rows, cols, dtype=BF):
    return jax.ShapeDtypeStruct((rows, cols), dtype)


def after(value, *others):
    return lax.optimization_barrier((value, *others))[0]


def spread(parts, gates=(None,) * 4):
    out = [None] * 8
    for t in range(4):
        part = parts[t] if gates[t] is None else after(parts[t], gates[t])
        out[2 * t] = part if t == 0 else swap(part, 2 * t, "seq")
    for t in range(4):
        out[2 * t + 1] = swap(out[2 * t], 1, "seq")
    return out


def to_owner_chip(value):
    reps, seq = lax.axis_size("rep"), lax.axis_size("seq")
    pairs = [
        ((2 * a + c) * reps + r, (2 * ((a ^ r) % 4) + c) * reps + r)
        for r in range(reps)
        for a in range(seq // 2)
        for c in range(2)
    ]
    return lax.ppermute(value, ("seq", "rep"), pairs)


def local_heads(signal, w_qkv, w_out, offsets, d_result):
    sig, grad = signal[0], d_result[0]
    reps = lax.axis_size("rep")
    pays = vmem_call(
        pack_kernel,
        [pltpu.with_memory_space_constraint(x, pltpu.HBM) for x in (sig, grad, w_qkv)],
        [shape(PAY, 128)] * 4,
        scratch=[
            pltpu.VMEM((TD, DM), BF),
            pltpu.VMEM((TD, DM), BF),
            pltpu.VMEM((HD, 3 * DM), BF),
            pltpu.SemaphoreType.DMA((3,)),
        ],
        raw=3,
    )
    S = spread(pays)
    scr = [pltpu.VMEM((1024, 128), F32)]
    res = vmem_call(
        functools.partial(head_kernel, reps),
        (offsets, *S, w_out),
        [shape(4 * TD, 256)] * 2
        + [shape(DM, 384), shape(2 * TD, 128, F32)]
        + [shape(2 * TD, 128)] * (reps - 1),
        scratch=scr * 6 + [pltpu.VMEM((256, DM), F32)],
        flops=10**9,
        smem=1,
    )
    keep, give, w_both, own, *chunks = res
    arrived = [swap(chunks[j - 1], j, "rep") for j in range(1, reps)]
    Y = vmem_call(
        project_kernel,
        (keep, swap(give, 1, "seq"), w_both, w_out, swap(w_out, 1, "seq")),
        [shape(TD, 2 * DM, F32)] + [shape(TD, 2 * DM)] * 3,
        flops=5 * 10**8,
    )
    own = after(own, *Y)
    total, dwo_part = vmem_call(
        sum_kernel, (own, *arrived), [shape(3 * HD, 128), shape(HD, 128)]
    )
    Y = [*Y[:3], after(Y[3], total)]
    Y = [Y[0]] + [swap(Y[t], 2 * t, "seq") for t in range(1, 4)]
    result, d_signal = vmem_call(add_kernel, Y, [shape(TD, DM)] * 2)
    rows = jnp.concatenate([to_owner_chip(total), dwo_part], axis=0)
    F = []
    for j in range(reps):
        same = swap(rows, j, "rep") if j else rows
        F += [same, swap(after(same, result) if j == reps - 1 else same, 1, "seq")]
    dw, dwo = vmem_call(
        total_kernel,
        F,
        [shape(HD, 3 * DM, F32), shape(HD, DM, F32)],
    )
    return (result[None], d_signal[None], dw, dwo)


def solution(mesh):
    in_specs = (P("rep", "seq", None), P("seq", None), P("seq", None), P(), P("rep", "seq", None))
    out_specs = (P("rep", "seq", None), P("rep", "seq", None), P("seq", None), P("seq", None))

    def body(signal, w_qkv, w_out, offsets, d_result):
        reps = mesh.shape["rep"]
        per_head = mesh.shape["seq"] == HEADS and reps == 4
        if per_head and signal.shape == (1, TD, DM) and w_qkv.shape == (HD, 3 * DM):
            return local_heads(signal, w_qkv, w_out, offsets, d_result)
        return local(signal, w_qkv, w_out, offsets, d_result)

    return jax.shard_map(body, mesh=mesh, in_specs=in_specs, out_specs=out_specs, check_vma=False)
```

```python
import functools
import math

import jax
import jax.numpy as jnp
from jax import lax
from jax.experimental import pallas as pl
from jax.experimental.pallas import tpu as pltpu
from jax.sharding import PartitionSpec as P

HEADS = 8


def from_partner(value, axis, stride):
    mask = 2**stride
    pairs = [(source, source ^ mask) for source in range(lax.axis_size(axis))]
    return lax.ppermute(value, axis, pairs)


def normalize(tensor):
    widened = tensor.astype(jnp.float32)
    factor = lax.rsqrt(jnp.mean(widened * widened, axis=-1, keepdims=True) + 1e-06)
    return (widened * factor, factor)


def gather_row_subset(full_row_tensor, dilation_step, start_shift):
    row_total = full_row_tensor.shape[0] // dilation_step
    reshaped_tensor = full_row_tensor.reshape(
        row_total, dilation_step, full_row_tensor.shape[1], full_row_tensor.shape[2]
    )
    chosen_rows_list = jnp.arange(dilation_step)[:, None] == start_shift[None, :]
    kept_rows = jnp.where(
        chosen_rows_list[None, :, :, None], reshaped_tensor, jnp.zeros((), full_row_tensor.dtype)
    )
    return jnp.sum(kept_rows, axis=1)


def scatter_row_subset(gathered_rows, dilation_step, start_shift):
    row_total, head_total, feature_count = gathered_rows.shape
    chosen_rows_list = jnp.arange(dilation_step)[:, None] == start_shift[None, :]
    scattered_rows = jnp.where(
        chosen_rows_list[None, :, :, None],
        gathered_rows[:, None],
        jnp.zeros((), gathered_rows.dtype),
    )
    return scattered_rows.reshape(row_total * dilation_step, head_total, feature_count)


def join_halves(own_part, peer_part, upper_bit):
    return jnp.where(
        upper_bit == 1,
        jnp.concatenate([peer_part, own_part], axis=0),
        jnp.concatenate([own_part, peer_part], axis=0),
    )


def attend(query_matrix, key_matrix_rows, value_matrix_rows, logit_scale):
    scores = (
        jnp.einsum(
            "ryk,oyk->yro", query_matrix, key_matrix_rows, preferred_element_type=jnp.float32
        )
        * logit_scale
    )
    exp_scores = jnp.exp(scores)
    softmax_denominator = jnp.sum(exp_scores, axis=-1).T
    softmax_numerator = jnp.einsum(
        "tcg,gto->cto",
        exp_scores.astype(jnp.bfloat16),
        value_matrix_rows,
        preferred_element_type=jnp.float32,
    )
    return (softmax_numerator, softmax_denominator)


def attend_back(
    query_matrix,
    key_matrix_rows,
    value_matrix_rows,
    gradient_rows,
    correction_rows,
    denom_rows,
    logit_scale,
):
    scores = (
        jnp.einsum(
            "ryk,oyk->yro", query_matrix, key_matrix_rows, preferred_element_type=jnp.float32
        )
        * logit_scale
    )
    prob_full = jnp.exp(scores) / denom_rows.T[:, :, None]
    value_gradient = jnp.einsum(
        "jvy,vjk->yjk",
        prob_full.astype(jnp.bfloat16),
        gradient_rows,
        preferred_element_type=jnp.float32,
    )
    probability_gradient = jnp.einsum(
        "ryk,oyk->yro", gradient_rows, value_matrix_rows, preferred_element_type=jnp.float32
    )
    score_gradient = (prob_full * (probability_gradient - correction_rows.T[:, :, None])).astype(
        jnp.bfloat16
    )
    d_query = (
        jnp.einsum(
            "tcg,gto->cto", score_gradient, key_matrix_rows, preferred_element_type=jnp.float32
        )
        * logit_scale
    )
    d_key = (
        jnp.einsum("jvy,vjk->yjk", score_gradient, query_matrix, preferred_element_type=jnp.float32)
        * logit_scale
    )
    return (d_query, d_key, value_gradient)


def local(signal, w_qkv, w_out, offsets, d_result):
    tok_rows = signal[0]
    upstream = d_result[0]
    t_dev, model_dim = tok_rows.shape
    head_total = HEADS
    head_dim = model_dim // head_total
    logit_scale = 1.0 / math.sqrt(head_dim)
    shards = lax.axis_size("seq")
    mid_rate = min(16, shards)
    mid_bits = mid_rate.bit_length() - 1
    shard_index = lax.axis_index("seq")
    mid_off = offsets[0]
    far_off = offsets[1]
    qkv_full, out_full = (
        lax.all_gather(w_qkv, "seq", axis=0, tiled=True),
        lax.all_gather(w_out, "seq", axis=0, tiled=True),
    )
    projected = jnp.dot(tok_rows, qkv_full, preferred_element_type=jnp.float32)
    qkv_rows = projected.astype(jnp.bfloat16)
    query_rows = qkv_rows[:, :model_dim].reshape(t_dev, head_total, head_dim)
    key_matrix_rows = qkv_rows[:, model_dim : 2 * model_dim].reshape(t_dev, head_total, head_dim)
    value_matrix_rows = qkv_rows[:, 2 * model_dim :].reshape(t_dev, head_total, head_dim)
    q_wide, q_factor = normalize(query_rows)
    k_wide, k_factor = normalize(key_matrix_rows)
    query_normalized = q_wide.astype(jnp.bfloat16)
    key_normalized = k_wide.astype(jnp.bfloat16)
    numer_near, denom_near = attend(
        query_normalized, key_normalized, value_matrix_rows, logit_scale
    )
    key_value = jnp.concatenate([key_normalized, value_matrix_rows], axis=2)
    mid_local = gather_row_subset(key_value, mid_rate, mid_off)
    far_local = gather_row_subset(key_value, shards, far_off)
    mid_all = mid_local
    for bit_num in range(mid_bits):
        partner = from_partner(mid_all, "seq", bit_num)
        mid_all = join_halves(mid_all, partner, shard_index // (1 << bit_num) % 2)
    far_all = lax.all_gather(far_local, "seq", axis=0, tiled=True)
    mid_keys_all = mid_all[..., :head_dim]
    mid_vals_all = mid_all[..., head_dim:]
    far_keys_all = far_all[..., :head_dim]
    far_vals_all = far_all[..., head_dim:]
    q_mid = gather_row_subset(query_normalized, mid_rate, mid_off)
    q_far = gather_row_subset(query_normalized, shards, far_off)
    numer_mid, denom_mid = attend(q_mid, mid_keys_all, mid_vals_all, logit_scale)
    numer_far, denom_far = attend(q_far, far_keys_all, far_vals_all, logit_scale)
    softmax_numerator = (
        numer_near
        + scatter_row_subset(numer_mid, mid_rate, mid_off)
        + scatter_row_subset(numer_far, shards, far_off)
    )
    softmax_denominator = (
        denom_near
        + scatter_row_subset(denom_mid[..., None], mid_rate, mid_off)[..., 0]
        + scatter_row_subset(denom_far[..., None], shards, far_off)[..., 0]
    )
    attn_three = (softmax_numerator / softmax_denominator[..., None]).astype(jnp.bfloat16)
    attn_rows = attn_three.reshape(t_dev, model_dim)
    layer_out = jnp.dot(attn_rows, out_full, preferred_element_type=jnp.float32)
    d_attn_wide = jnp.dot(upstream, out_full.T, preferred_element_type=jnp.float32)
    result = layer_out.astype(jnp.bfloat16)
    attention_gradient = d_attn_wide.astype(jnp.bfloat16).reshape(t_dev, head_total, head_dim)
    correction_rows = jnp.sum(
        attention_gradient.astype(jnp.float32) * attn_three.astype(jnp.float32), axis=-1
    )
    dq_near, dk_near, dv_near = attend_back(
        query_normalized,
        key_normalized,
        value_matrix_rows,
        attention_gradient,
        correction_rows,
        softmax_denominator,
        logit_scale,
    )
    g_mid = gather_row_subset(attention_gradient, mid_rate, mid_off)
    g_far = gather_row_subset(attention_gradient, shards, far_off)
    delta_mid = gather_row_subset(correction_rows[..., None], mid_rate, mid_off)[..., 0]
    delta_far = gather_row_subset(correction_rows[..., None], shards, far_off)[..., 0]
    denom_mid_q = gather_row_subset(softmax_denominator[..., None], mid_rate, mid_off)[..., 0]
    denom_far_q = gather_row_subset(softmax_denominator[..., None], shards, far_off)[..., 0]
    dq_mid, dk_mid_part, dv_mid_part = attend_back(
        q_mid, mid_keys_all, mid_vals_all, g_mid, delta_mid, denom_mid_q, logit_scale
    )
    dq_far, dk_far_part, dv_far_part = attend_back(
        q_far, far_keys_all, far_vals_all, g_far, delta_far, denom_far_q, logit_scale
    )
    query_pack = jnp.concatenate([q_mid, g_mid], axis=2)
    stat_pack = jnp.stack([delta_mid, denom_mid_q], axis=2)
    for bit_num in range(mid_bits):
        upper_bit = shard_index // (1 << bit_num) % 2
        peer_query = from_partner(query_pack, "seq", bit_num)
        peer_stats = from_partner(stat_pack, "seq", bit_num)
        query_pack = join_halves(query_pack, peer_query, upper_bit)
        stat_pack = join_halves(stat_pack, peer_stats, upper_bit)
    unused_mid, dk_mid, dv_mid = attend_back(
        query_pack[..., :head_dim],
        mid_local[..., :head_dim],
        mid_local[..., head_dim:],
        query_pack[..., head_dim:],
        stat_pack[..., 0],
        stat_pack[..., 1],
        logit_scale,
    )
    far_query_pack = lax.all_gather(
        jnp.concatenate([q_far, g_far], axis=2), "seq", axis=0, tiled=True
    )
    far_stat_pack = lax.all_gather(
        jnp.stack([delta_far, denom_far_q], axis=2), "seq", axis=0, tiled=True
    )
    unused_far, dk_far, dv_far = attend_back(
        far_query_pack[..., :head_dim],
        far_local[..., :head_dim],
        far_local[..., head_dim:],
        far_query_pack[..., head_dim:],
        far_stat_pack[..., 0],
        far_stat_pack[..., 1],
        logit_scale,
    )
    normed_query_gradient = (
        dq_near
        + scatter_row_subset(dq_mid, mid_rate, mid_off)
        + scatter_row_subset(dq_far, shards, far_off)
    )
    normed_key_gradient = (
        dk_near
        + scatter_row_subset(dk_mid, mid_rate, mid_off)
        + scatter_row_subset(dk_far, shards, far_off)
    )
    value_gradient = (
        dv_near
        + scatter_row_subset(dv_mid, mid_rate, mid_off)
        + scatter_row_subset(dv_far, shards, far_off)
    )
    d_query = q_factor * (
        normed_query_gradient
        - q_wide * jnp.mean(normed_query_gradient * q_wide, axis=-1, keepdims=True)
    )
    d_key = k_factor * (
        normed_key_gradient
        - k_wide * jnp.mean(normed_key_gradient * k_wide, axis=-1, keepdims=True)
    )
    d_qkv = jnp.concatenate(
        [
            d_query.reshape(t_dev, model_dim),
            d_key.reshape(t_dev, model_dim),
            value_gradient.reshape(t_dev, model_dim),
        ],
        axis=1,
    ).astype(jnp.bfloat16)
    d_input = jnp.dot(d_qkv, qkv_full.T, preferred_element_type=jnp.float32)
    d_signal = d_input.astype(jnp.bfloat16)
    grad_in = jnp.einsum("ti,tj->ij", tok_rows, d_qkv, preferred_element_type=jnp.float32)
    grad_mix = jnp.einsum("ti,tj->ij", attn_rows, upstream, preferred_element_type=jnp.float32)
    owned = lax.psum_scatter(
        jnp.concatenate([grad_in, grad_mix], axis=1), "seq", scatter_dimension=0, tiled=True
    )
    owned = lax.psum(owned, "rep")
    return (result[None], d_signal[None], owned[:, : 3 * model_dim], owned[:, 3 * model_dim :])


BF = jnp.bfloat16
F32 = jnp.float32
TD = 128
HD = 64
DM = 512
NN = (((1,), (0,)), ((), ()))
NT = (((1,), (1,)), ((), ()))
TN = (((0,), (0,)), ((), ()))


def mm(a, b, dims=NN):
    return lax.dot_general(a, b, dims, preferred_element_type=F32)


def low_lanes(rows):
    return lax.broadcasted_iota(jnp.int32, (rows, 128), 1) < HD


def swap_halves(tile):
    return pltpu.roll(tile.astype(F32), HD, 1)


W_ROWS = 3 * HD
TILES = 4 * TD


def pack_kernel(sig_ref, grad_ref, wqkv_ref, pay0, pay1, pay2, s_scr, d_scr, w_scr, sems):
    chip = lax.axis_index("seq") // 2
    low = low_lanes(HD)
    loads = [
        pltpu.make_async_copy(src, dst, sems.at[n])
        for n, (src, dst) in enumerate(((wqkv_ref, w_scr), (sig_ref, s_scr), (grad_ref, d_scr)))
    ]
    for load in loads:
        load.start()
    loads[0].wait()
    pays = ((pay0, W_ROWS), (pay1, W_ROWS), (pay2, 2 * W_ROWS))
    for t, (pay, at) in enumerate((*((pay, 0) for pay, _ in pays), (pay2, W_ROWS))):
        col = (chip ^ t) * 128
        q = w_scr[:, pl.ds(pl.multiple_of(col, 128), 128)].astype(F32)
        k = w_scr[:, pl.ds(pl.multiple_of(DM + col, 128), 128)].astype(F32)
        pay[at : at + HD, :] = jnp.where(low, q, swap_halves(k)).astype(BF)
        pay[at + HD : at + 2 * HD, :] = jnp.where(low, swap_halves(q), k).astype(BF)
        pay[at + 2 * HD : at + W_ROWS, :] = w_scr[:, pl.ds(pl.multiple_of(2 * DM + col, 128), 128)]
    for scr, load, shift in ((s_scr, loads[1], 0), (d_scr, loads[2], TILES)):
        load.wait()
        for pay, at in pays:
            for n in range(4):
                row = at + shift + TD * n
                pay[row : row + TD, :] = scr[:, 128 * n : 128 * n + 128]


def tiles(*runs):
    parts = [ref[at + TD * n : at + TD * n + TD, :] for ref, at, count in runs for n in range(count)]
    return jnp.concatenate(parts, axis=1)


def stack(parts):
    return jnp.concatenate(parts, axis=0)


def halves(values):
    head = values.astype(BF)
    return jnp.concatenate([head, (values - head.astype(F32)).astype(BF)], axis=1)


def lanes_where(rows, test):
    a = lax.broadcasted_iota(jnp.int32, (rows, 128), 0) % 128
    b = lax.broadcasted_iota(jnp.int32, (rows, 128), 1)
    return test(a, b).astype(F32).astype(BF)


def head_kernel(reps, off_ref, *refs):
    own, mate, x_own, x_mate, y_own, y_mate, far_a, far_b, far_a_mate, far_b_mate, wo_ref = refs[0:11]
    S = (own, mate, x_own, x_mate, y_own, y_mate, far_a, far_a_mate)
    starts = [W_ROWS] * 4 + [2 * W_ROWS] * 2
    x_runs = [[(S[m], at, 4)] for m, at in enumerate(starts)]
    d_runs = [[(S[m], at + TILES, 4)] for m, at in enumerate(starts)]
    for a, b in ((far_a, far_b), (far_a_mate, far_b_mate)):
        x_runs.append([(a, W_ROWS, 2), (b, 0, 2)])
        d_runs.append([(b, 2 * TD, 4)])
    keep_ref, give_ref, w_ref, own_ref, chunks = *refs[11:15], refs[15 : 14 + reps]
    qk_scr, v_scr, acc_scr, g_scr, dq_scr, dvk_scr, dw_scr = refs[14 + reps :]
    me = lax.axis_index("seq")
    chip, core, rep = me // 2, me % 2, lax.axis_index("rep")
    scale = 1.0 / math.sqrt(HD)
    low = low_lanes(TD)
    same_half = lanes_where(256, lambda a, b: (a < HD) == (b < HD))
    low_to_high = lanes_where(256, lambda a, b: (a < HD) & (b >= HD))
    ones_high = lanes_where(TD, lambda a, b: b >= HD)
    blocks = [slice(TD * m, TD * m + TD) for m in range(8)]
    picks = [pl.ds(off_ref[level, me], TD, stride=8) for level in range(2)]

    def spread_high(tile):
        return jnp.where(low, swap_halves(tile), tile)

    for m in range(8):
        rows = pl.ds(pl.multiple_of((me ^ m) * HD, HD), HD)
        w_ref[rows, 0:128] = S[m][pl.ds(pl.multiple_of(core * HD, HD), HD), :]
        w_ref[rows, 128:256] = S[m][2 * HD : W_ROWS, :]
        w_ref[rows, 256:384] = S[m][pl.ds(pl.multiple_of((1 - core) * HD, HD), HD), :]
    x = stack([tiles(*runs) for runs in x_runs])
    upstream = stack([tiles(*runs) for runs in d_runs])
    wide = stack([wo_ref[...], jnp.zeros((HD, DM), BF)])
    da = mm(upstream, wide, NT).astype(BF)
    qkv = mm(x, w_ref[:, 0:256]).astype(BF).astype(F32)
    qk, pair = qkv[:, 0:128], qkv[:, 128:256]
    vv = jnp.where(core == 1, swap_halves(pair), pair)
    rho = lax.rsqrt(mm(halves(qk * qk), same_half) * (1.0 / HD) + 1e-6)
    qkw = qk * rho
    qkn = qkw.astype(BF).astype(F32)
    qk_scr[...] = qkn
    v_scr[...] = vv
    flipped = swap_halves(qkn)

    def forward(qkn, flipped, vv):
        s = mm(qkn[:, :HD].astype(BF), flipped[:, :HD].astype(BF), NT)
        return jnp.exp(s * scale)

    def weigh(e, vv):
        right = stack([jnp.where(low, vv, 1.0).astype(BF), ones_high])
        return mm(halves(e), right)

    near = [forward(qkn[b], flipped[b], vv[b]) for b in blocks]
    for b, e in zip(blocks, near):
        acc_scr[b, :] = weigh(e, vv[b])
    far = [(qk_scr[pick, :], v_scr[pick, :]) for pick in picks]
    far = [(q, swap_halves(q), v) for q, v in far]
    far_e = [forward(*tiles) for tiles in far]
    for pick, e, (_, _, v) in zip(picks, far_e, far):
        acc_scr[pick, :] = acc_scr[pick, :] + weigh(e, v)

    accs = [acc_scr[b, :] for b in blocks]
    rdens = [1.0 / spread_high(acc) for acc in accs]
    attns = [jnp.where(low, acc * r, 0.0).astype(BF) for acc, r in zip(accs, rdens)]
    dot_terms = da.astype(F32) * stack(attns).astype(F32)
    grads = da.astype(F32) + mm(halves(dot_terms), low_to_high)
    g_scr[...] = grads

    def backward(e, rden, flipped, vv, da, delta):
        prob = e * rden
        dp = mm(da, vv.astype(BF), NT)
        ds = (prob * (dp - delta)).astype(BF)
        dq = mm(ds, flipped.astype(BF))
        qz = jnp.where(low, 0.0, flipped).astype(BF)
        return dq, mm(stack([prob.astype(BF), ds]), stack([da, qz]), TN)

    for m, b in enumerate(blocks):
        dq, dvk = backward(
            near[m], rdens[m], flipped[b], vv[b], da[b], spread_high(grads[b])
        )
        dq_scr[b, :] = dq
        dvk_scr[b, :] = dvk
    for pick, e, (_, f, v) in zip(picks, far_e, far):
        g = g_scr[pick, :]
        dq, dvk = backward(
            e,
            1.0 / spread_high(acc_scr[pick, :]),
            f,
            v,
            jnp.where(low, g, 0.0).astype(BF),
            spread_high(g),
        )
        dq_scr[pick, :] = dq_scr[pick, :] + dq
        dvk_scr[pick, :] = dvk_scr[pick, :] + dvk

    low_all = low_lanes(1024)
    dvk = dvk_scr[...]
    dqk = jnp.where(low_all, dq_scr[...], dvk) * scale
    mean = mm(halves(dqk * qkw), same_half) * (1.0 / HD)
    dqk = (rho * (dqk - qkw * mean)).astype(BF)
    attn_high = swap_halves(stack(attns))
    tile = jnp.concatenate([dqk, jnp.where(low_all, dvk, attn_high).astype(BF)], axis=1)
    for m, b in enumerate(blocks):
        ref = give_ref if m % 2 else keep_ref
        ref[TD * (m // 2) : TD * (m // 2) + TD, :] = tile[b]
    dw_scr[0 : 3 * HD, :] = mm(tile[:, 0 : 3 * HD], x, TN)
    dw_scr[3 * HD :, :] = mm(stack(attns), upstream, TN)[:HD]
    for j in range(reps):
        ref = chunks[j - 1] if j else own_ref
        at = pl.multiple_of(((chip ^ rep ^ j) % 4) * TD, TD)
        ref[...] = dw_scr[:, pl.ds(at, 128)].astype(ref.dtype)


def project_kernel(keep_ref, got_ref, w_ref, wo_ref, wo_mate_ref, *outs):
    core = lax.axis_index("seq") % 2
    low = low_lanes(TD)
    wo = jnp.concatenate([wo_ref[...], wo_mate_ref[...]], axis=0)
    for t, out in enumerate(outs):
        rows = slice(TD * t, TD * t + TD)
        a, b = keep_ref[rows, 128:256].astype(F32), got_ref[rows, 128:256].astype(F32)
        attn = jnp.where(low, pltpu.roll(a, HD, 1), b).astype(BF)
        even, odd = jnp.where(core == 1, b, a), jnp.where(core == 1, a, b)
        dv = jnp.where(low, even, pltpu.roll(odd, HD, 1)).astype(BF)
        d_all = jnp.concatenate([keep_ref[rows, 0:128], dv, got_ref[rows, 0:128]], axis=1)
        out[:, 0:DM] = mm(attn, wo).astype(out.dtype)
        out[:, DM:] = mm(d_all, w_ref[...], NT).astype(out.dtype)


def add_kernel(*refs):
    total = refs[0][...].astype(F32)
    for ref in refs[1:-2]:
        total = total + ref[...].astype(F32)
    refs[-2][...] = total[:, 0:DM].astype(BF)
    refs[-1][...] = total[:, DM:].astype(BF)


def sum_kernel(*refs):
    total = refs[0][...]
    for ref in refs[1:-2]:
        total = total + ref[...].astype(F32)
    dv = total[TD : 3 * HD]
    turned = stack([dv, dv]).T
    refs[-2][0:TD, :] = total[0:TD].T.astype(BF)
    refs[-2][TD:, :] = jnp.where(low_lanes(HD), turned[:HD], turned[HD:]).astype(BF)
    refs[-1][...] = total[3 * HD :].astype(BF)


def total_kernel(*refs):
    F, (dw_ref, dwo_ref) = refs[:-2], refs[-2:]
    me = lax.axis_index("seq")
    chip, core = me // 2, me % 2
    rep = lax.axis_index("rep")
    low = low_lanes(HD)
    mine = pl.ds(pl.multiple_of(core * HD, HD), HD)
    for j in range(4):
        col = ((chip ^ rep ^ j) % 4) * 128
        a, b = F[2 * j], F[2 * j + 1]
        aqk, bqk = a[mine, :].astype(F32), b[mine, :].astype(F32)
        av, bv = a[TD : 3 * HD, :].astype(F32), b[TD : 3 * HD, :].astype(F32)
        even, odd = jnp.where(core == 1, bqk, aqk), jnp.where(core == 1, aqk, bqk)
        v = jnp.where(
            low,
            jnp.where(core == 1, pltpu.roll(bv, HD, 1), av),
            jnp.where(core == 1, av, pltpu.roll(bv, HD, 1)),
        )
        tiles = (
            jnp.where(low, even, pltpu.roll(odd, HD, 1)),
            jnp.where(low, pltpu.roll(even, HD, 1), odd),
            v,
        )
        for part, tile in enumerate(tiles):
            dw_ref[:, pl.ds(pl.multiple_of(part * DM + col, 128), 128)] = tile
        dwo_ref[:, pl.ds(pl.multiple_of(col, 128), 128)] = a[3 * HD :, :].astype(F32)


def vmem_call(body, ins, outs, scratch=(), flops=0, smem=0, raw=0):
    bytes_moved = sum(x.size * x.dtype.itemsize for x in list(ins) + list(outs))
    vmem = pl.BlockSpec(memory_space=pltpu.VMEM)
    specs = [pl.BlockSpec(memory_space=pltpu.SMEM)] * smem + [pl.BlockSpec(memory_space=pltpu.HBM)] * raw
    return pl.pallas_call(
        body,
        out_shape=list(outs),
        in_specs=specs + [vmem] * (len(ins) - smem - raw),
        out_specs=[vmem] * len(outs),
        scratch_shapes=list(scratch),
        compiler_params=pltpu.CompilerParams(vmem_limit_bytes=24 << 20),
        cost_estimate=pl.CostEstimate(flops=flops, bytes_accessed=bytes_moved, transcendentals=0),
    )(*ins)


def swap(value, mask, axis):
    return lax.ppermute(value, axis, [(i, i ^ mask) for i in range(lax.axis_size(axis))])


def shape(rows, cols, dtype=BF):
    return jax.ShapeDtypeStruct((rows, cols), dtype)


def after(value, *others):
    return lax.optimization_barrier((value, *others))[0]


def to_owner_chip(value):
    reps, seq = lax.axis_size("rep"), lax.axis_size("seq")
    pairs = [
        ((2 * a + c) * reps + r, (2 * ((a ^ r) % 4) + c) * reps + r)
        for r in range(reps)
        for a in range(seq // 2)
        for c in range(2)
    ]
    return lax.ppermute(value, ("seq", "rep"), pairs)


def local_heads(signal, w_qkv, w_out, offsets, d_result):
    sig, grad = signal[0], d_result[0]
    reps = lax.axis_size("rep")
    pays = vmem_call(
        pack_kernel,
        [pltpu.with_memory_space_constraint(x, pltpu.HBM) for x in (sig, grad, w_qkv)],
        [shape(W_ROWS + 2 * TILES, 128)] * 2 + [shape(2 * W_ROWS + 2 * TILES, 128)],
        scratch=[
            pltpu.VMEM((TD, DM), BF),
            pltpu.VMEM((TD, DM), BF),
            pltpu.VMEM((HD, 3 * DM), BF),
            pltpu.SemaphoreType.DMA((3,)),
        ],
        raw=3,
    )
    x_own = swap(pays[1], 2, "seq")
    y_own = swap(pays[2], 4, "seq")
    far_b = swap(x_own[W_ROWS + 2 * TD :], 4, "seq")
    far_a = swap(y_own[W_ROWS : 2 * W_ROWS + 2 * TD], 2, "seq")
    S = [pays[0], swap(pays[0], 1, "seq"), x_own, swap(x_own, 1, "seq"), y_own, swap(y_own, 1, "seq")]
    S += [far_a, far_b, swap(far_a, 1, "seq"), swap(far_b, 1, "seq")]
    wo_mate = swap(w_out, 1, "seq")
    scr = [pltpu.VMEM((1024, 128), F32)]
    res = vmem_call(
        functools.partial(head_kernel, reps),
        (offsets, *S, w_out),
        [shape(4 * TD, 256)] * 2
        + [shape(DM, 384), shape(2 * TD, 128, F32)]
        + [shape(2 * TD, 128)] * (reps - 1),
        scratch=scr * 6 + [pltpu.VMEM((256, DM), F32)],
        flops=10**9,
        smem=1,
    )
    keep, give, w_both, own, *chunks = res
    got = swap(give, 1, "seq")
    chunks[0] = after(chunks[0], got)
    arrived = [swap(chunks[j - 1], j, "rep") for j in range(1, reps)]
    Y = vmem_call(
        project_kernel,
        (keep, got, w_both, w_out, wo_mate),
        [shape(TD, 2 * DM, F32)] + [shape(TD, 2 * DM)] * 3,
        flops=5 * 10**8,
    )
    own = after(own, *Y)
    total, dwo_part = vmem_call(
        sum_kernel, (own, *arrived), [shape(3 * HD, 128), shape(HD, 128)]
    )
    Y = [*Y[:3], after(Y[3], total)]
    Y = [Y[0]] + [swap(Y[t], 2 * t, "seq") for t in range(1, 4)]
    result, d_signal = vmem_call(add_kernel, Y, [shape(TD, DM)] * 2)
    rows = jnp.concatenate([to_owner_chip(total), dwo_part], axis=0)
    F = []
    for j in range(reps):
        same = swap(rows, j, "rep") if j else rows
        F += [same, swap(after(same, result) if j == reps - 1 else same, 1, "seq")]
    dw, dwo = vmem_call(
        total_kernel,
        F,
        [shape(HD, 3 * DM, F32), shape(HD, DM, F32)],
    )
    return (result[None], d_signal[None], dw, dwo)


def solution(mesh):
    in_specs = (P("rep", "seq", None), P("seq", None), P("seq", None), P(), P("rep", "seq", None))
    out_specs = (P("rep", "seq", None), P("rep", "seq", None), P("seq", None), P("seq", None))

    def body(signal, w_qkv, w_out, offsets, d_result):
        reps = mesh.shape["rep"]
        per_head = mesh.shape["seq"] == HEADS and reps == 4
        if per_head and signal.shape == (1, TD, DM) and w_qkv.shape == (HD, 3 * DM):
            return local_heads(signal, w_qkv, w_out, offsets, d_result)
        return local(signal, w_qkv, w_out, offsets, d_result)

    return jax.shard_map(body, mesh=mesh, in_specs=in_specs, out_specs=out_specs, check_vma=False)
```

```python
import functools
import math

import jax
import jax.numpy as jnp
from jax import lax
from jax.experimental import pallas as pl
from jax.experimental.pallas import tpu as pltpu
from jax.sharding import PartitionSpec as P

HEADS = 8


def from_partner(value, axis, stride):
    mask = 2**stride
    pairs = [(source, source ^ mask) for source in range(lax.axis_size(axis))]
    return lax.ppermute(value, axis, pairs)


def normalize(tensor):
    widened = tensor.astype(jnp.float32)
    factor = lax.rsqrt(jnp.mean(widened * widened, axis=-1, keepdims=True) + 1e-06)
    return (widened * factor, factor)


def gather_row_subset(full_row_tensor, dilation_step, start_shift):
    row_total = full_row_tensor.shape[0] // dilation_step
    reshaped_tensor = full_row_tensor.reshape(
        row_total, dilation_step, full_row_tensor.shape[1], full_row_tensor.shape[2]
    )
    chosen_rows_list = jnp.arange(dilation_step)[:, None] == start_shift[None, :]
    kept_rows = jnp.where(
        chosen_rows_list[None, :, :, None], reshaped_tensor, jnp.zeros((), full_row_tensor.dtype)
    )
    return jnp.sum(kept_rows, axis=1)


def scatter_row_subset(gathered_rows, dilation_step, start_shift):
    row_total, head_total, feature_count = gathered_rows.shape
    chosen_rows_list = jnp.arange(dilation_step)[:, None] == start_shift[None, :]
    scattered_rows = jnp.where(
        chosen_rows_list[None, :, :, None],
        gathered_rows[:, None],
        jnp.zeros((), gathered_rows.dtype),
    )
    return scattered_rows.reshape(row_total * dilation_step, head_total, feature_count)


def join_halves(own_part, peer_part, upper_bit):
    return jnp.where(
        upper_bit == 1,
        jnp.concatenate([peer_part, own_part], axis=0),
        jnp.concatenate([own_part, peer_part], axis=0),
    )


def attend(query_matrix, key_matrix_rows, value_matrix_rows, logit_scale):
    scores = (
        jnp.einsum(
            "ryk,oyk->yro", query_matrix, key_matrix_rows, preferred_element_type=jnp.float32
        )
        * logit_scale
    )
    exp_scores = jnp.exp(scores)
    softmax_denominator = jnp.sum(exp_scores, axis=-1).T
    softmax_numerator = jnp.einsum(
        "tcg,gto->cto",
        exp_scores.astype(jnp.bfloat16),
        value_matrix_rows,
        preferred_element_type=jnp.float32,
    )
    return (softmax_numerator, softmax_denominator)


def attend_back(
    query_matrix,
    key_matrix_rows,
    value_matrix_rows,
    gradient_rows,
    correction_rows,
    denom_rows,
    logit_scale,
):
    scores = (
        jnp.einsum(
            "ryk,oyk->yro", query_matrix, key_matrix_rows, preferred_element_type=jnp.float32
        )
        * logit_scale
    )
    prob_full = jnp.exp(scores) / denom_rows.T[:, :, None]
    value_gradient = jnp.einsum(
        "jvy,vjk->yjk",
        prob_full.astype(jnp.bfloat16),
        gradient_rows,
        preferred_element_type=jnp.float32,
    )
    probability_gradient = jnp.einsum(
        "ryk,oyk->yro", gradient_rows, value_matrix_rows, preferred_element_type=jnp.float32
    )
    score_gradient = (prob_full * (probability_gradient - correction_rows.T[:, :, None])).astype(
        jnp.bfloat16
    )
    d_query = (
        jnp.einsum(
            "tcg,gto->cto", score_gradient, key_matrix_rows, preferred_element_type=jnp.float32
        )
        * logit_scale
    )
    d_key = (
        jnp.einsum("jvy,vjk->yjk", score_gradient, query_matrix, preferred_element_type=jnp.float32)
        * logit_scale
    )
    return (d_query, d_key, value_gradient)


def local(signal, w_qkv, w_out, offsets, d_result):
    tok_rows = signal[0]
    upstream = d_result[0]
    t_dev, model_dim = tok_rows.shape
    head_total = HEADS
    head_dim = model_dim // head_total
    logit_scale = 1.0 / math.sqrt(head_dim)
    shards = lax.axis_size("seq")
    mid_rate = min(16, shards)
    mid_bits = mid_rate.bit_length() - 1
    shard_index = lax.axis_index("seq")
    mid_off = offsets[0]
    far_off = offsets[1]
    qkv_full, out_full = (
        lax.all_gather(w_qkv, "seq", axis=0, tiled=True),
        lax.all_gather(w_out, "seq", axis=0, tiled=True),
    )
    projected = jnp.dot(tok_rows, qkv_full, preferred_element_type=jnp.float32)
    qkv_rows = projected.astype(jnp.bfloat16)
    query_rows = qkv_rows[:, :model_dim].reshape(t_dev, head_total, head_dim)
    key_matrix_rows = qkv_rows[:, model_dim : 2 * model_dim].reshape(t_dev, head_total, head_dim)
    value_matrix_rows = qkv_rows[:, 2 * model_dim :].reshape(t_dev, head_total, head_dim)
    q_wide, q_factor = normalize(query_rows)
    k_wide, k_factor = normalize(key_matrix_rows)
    query_normalized = q_wide.astype(jnp.bfloat16)
    key_normalized = k_wide.astype(jnp.bfloat16)
    numer_near, denom_near = attend(
        query_normalized, key_normalized, value_matrix_rows, logit_scale
    )
    key_value = jnp.concatenate([key_normalized, value_matrix_rows], axis=2)
    mid_local = gather_row_subset(key_value, mid_rate, mid_off)
    far_local = gather_row_subset(key_value, shards, far_off)
    mid_all = mid_local
    for bit_num in range(mid_bits):
        partner = from_partner(mid_all, "seq", bit_num)
        mid_all = join_halves(mid_all, partner, shard_index // (1 << bit_num) % 2)
    far_all = lax.all_gather(far_local, "seq", axis=0, tiled=True)
    mid_keys_all = mid_all[..., :head_dim]
    mid_vals_all = mid_all[..., head_dim:]
    far_keys_all = far_all[..., :head_dim]
    far_vals_all = far_all[..., head_dim:]
    q_mid = gather_row_subset(query_normalized, mid_rate, mid_off)
    q_far = gather_row_subset(query_normalized, shards, far_off)
    numer_mid, denom_mid = attend(q_mid, mid_keys_all, mid_vals_all, logit_scale)
    numer_far, denom_far = attend(q_far, far_keys_all, far_vals_all, logit_scale)
    softmax_numerator = (
        numer_near
        + scatter_row_subset(numer_mid, mid_rate, mid_off)
        + scatter_row_subset(numer_far, shards, far_off)
    )
    softmax_denominator = (
        denom_near
        + scatter_row_subset(denom_mid[..., None], mid_rate, mid_off)[..., 0]
        + scatter_row_subset(denom_far[..., None], shards, far_off)[..., 0]
    )
    attn_three = (softmax_numerator / softmax_denominator[..., None]).astype(jnp.bfloat16)
    attn_rows = attn_three.reshape(t_dev, model_dim)
    layer_out = jnp.dot(attn_rows, out_full, preferred_element_type=jnp.float32)
    d_attn_wide = jnp.dot(upstream, out_full.T, preferred_element_type=jnp.float32)
    result = layer_out.astype(jnp.bfloat16)
    attention_gradient = d_attn_wide.astype(jnp.bfloat16).reshape(t_dev, head_total, head_dim)
    correction_rows = jnp.sum(
        attention_gradient.astype(jnp.float32) * attn_three.astype(jnp.float32), axis=-1
    )
    dq_near, dk_near, dv_near = attend_back(
        query_normalized,
        key_normalized,
        value_matrix_rows,
        attention_gradient,
        correction_rows,
        softmax_denominator,
        logit_scale,
    )
    g_mid = gather_row_subset(attention_gradient, mid_rate, mid_off)
    g_far = gather_row_subset(attention_gradient, shards, far_off)
    delta_mid = gather_row_subset(correction_rows[..., None], mid_rate, mid_off)[..., 0]
    delta_far = gather_row_subset(correction_rows[..., None], shards, far_off)[..., 0]
    denom_mid_q = gather_row_subset(softmax_denominator[..., None], mid_rate, mid_off)[..., 0]
    denom_far_q = gather_row_subset(softmax_denominator[..., None], shards, far_off)[..., 0]
    dq_mid, dk_mid_part, dv_mid_part = attend_back(
        q_mid, mid_keys_all, mid_vals_all, g_mid, delta_mid, denom_mid_q, logit_scale
    )
    dq_far, dk_far_part, dv_far_part = attend_back(
        q_far, far_keys_all, far_vals_all, g_far, delta_far, denom_far_q, logit_scale
    )
    query_pack = jnp.concatenate([q_mid, g_mid], axis=2)
    stat_pack = jnp.stack([delta_mid, denom_mid_q], axis=2)
    for bit_num in range(mid_bits):
        upper_bit = shard_index // (1 << bit_num) % 2
        peer_query = from_partner(query_pack, "seq", bit_num)
        peer_stats = from_partner(stat_pack, "seq", bit_num)
        query_pack = join_halves(query_pack, peer_query, upper_bit)
        stat_pack = join_halves(stat_pack, peer_stats, upper_bit)
    unused_mid, dk_mid, dv_mid = attend_back(
        query_pack[..., :head_dim],
        mid_local[..., :head_dim],
        mid_local[..., head_dim:],
        query_pack[..., head_dim:],
        stat_pack[..., 0],
        stat_pack[..., 1],
        logit_scale,
    )
    far_query_pack = lax.all_gather(
        jnp.concatenate([q_far, g_far], axis=2), "seq", axis=0, tiled=True
    )
    far_stat_pack = lax.all_gather(
        jnp.stack([delta_far, denom_far_q], axis=2), "seq", axis=0, tiled=True
    )
    unused_far, dk_far, dv_far = attend_back(
        far_query_pack[..., :head_dim],
        far_local[..., :head_dim],
        far_local[..., head_dim:],
        far_query_pack[..., head_dim:],
        far_stat_pack[..., 0],
        far_stat_pack[..., 1],
        logit_scale,
    )
    normed_query_gradient = (
        dq_near
        + scatter_row_subset(dq_mid, mid_rate, mid_off)
        + scatter_row_subset(dq_far, shards, far_off)
    )
    normed_key_gradient = (
        dk_near
        + scatter_row_subset(dk_mid, mid_rate, mid_off)
        + scatter_row_subset(dk_far, shards, far_off)
    )
    value_gradient = (
        dv_near
        + scatter_row_subset(dv_mid, mid_rate, mid_off)
        + scatter_row_subset(dv_far, shards, far_off)
    )
    d_query = q_factor * (
        normed_query_gradient
        - q_wide * jnp.mean(normed_query_gradient * q_wide, axis=-1, keepdims=True)
    )
    d_key = k_factor * (
        normed_key_gradient
        - k_wide * jnp.mean(normed_key_gradient * k_wide, axis=-1, keepdims=True)
    )
    d_qkv = jnp.concatenate(
        [
            d_query.reshape(t_dev, model_dim),
            d_key.reshape(t_dev, model_dim),
            value_gradient.reshape(t_dev, model_dim),
        ],
        axis=1,
    ).astype(jnp.bfloat16)
    d_input = jnp.dot(d_qkv, qkv_full.T, preferred_element_type=jnp.float32)
    d_signal = d_input.astype(jnp.bfloat16)
    grad_in = jnp.einsum("ti,tj->ij", tok_rows, d_qkv, preferred_element_type=jnp.float32)
    grad_mix = jnp.einsum("ti,tj->ij", attn_rows, upstream, preferred_element_type=jnp.float32)
    owned = lax.psum_scatter(
        jnp.concatenate([grad_in, grad_mix], axis=1), "seq", scatter_dimension=0, tiled=True
    )
    owned = lax.psum(owned, "rep")
    return (result[None], d_signal[None], owned[:, : 3 * model_dim], owned[:, 3 * model_dim :])


BF = jnp.bfloat16
F32 = jnp.float32
TD = 128
HD = 64
DM = 512
NN = (((1,), (0,)), ((), ()))
NT = (((1,), (1,)), ((), ()))
TN = (((0,), (0,)), ((), ()))


def mm(a, b, dims=NN):
    return lax.dot_general(a, b, dims, preferred_element_type=F32)


def low_lanes(rows):
    return lax.broadcasted_iota(jnp.int32, (rows, 128), 1) < HD


def swap_halves(tile):
    return pltpu.roll(tile.astype(F32), HD, 1)


W_ROWS = 3 * HD
TILES = 4 * TD


def pack_kernel(sig_ref, grad_ref, wqkv_ref, pay0, pay1, pay2, s_scr, d_scr, w_scr, sems):
    chip = lax.axis_index("seq") // 2
    low = low_lanes(HD)
    loads = [
        pltpu.make_async_copy(src, dst, sems.at[n])
        for n, (src, dst) in enumerate(((wqkv_ref, w_scr), (sig_ref, s_scr), (grad_ref, d_scr)))
    ]
    for load in loads:
        load.start()
    loads[0].wait()
    pays = ((pay0, W_ROWS), (pay1, W_ROWS), (pay2, 2 * W_ROWS))
    for t, (pay, at) in enumerate((*((pay, 0) for pay, _ in pays), (pay2, W_ROWS))):
        col = (chip ^ t) * 128
        q = w_scr[:, pl.ds(pl.multiple_of(col, 128), 128)].astype(F32)
        k = w_scr[:, pl.ds(pl.multiple_of(DM + col, 128), 128)].astype(F32)
        pay[at : at + HD, :] = jnp.where(low, q, swap_halves(k)).astype(BF)
        pay[at + HD : at + 2 * HD, :] = jnp.where(low, swap_halves(q), k).astype(BF)
        pay[at + 2 * HD : at + W_ROWS, :] = w_scr[:, pl.ds(pl.multiple_of(2 * DM + col, 128), 128)]
    for scr, load, shift in ((s_scr, loads[1], 0), (d_scr, loads[2], TILES)):
        load.wait()
        for pay, at in pays:
            for n in range(4):
                row = at + shift + TD * n
                pay[row : row + TD, :] = scr[:, 128 * n : 128 * n + 128]


def tiles(*runs):
    parts = [ref[at + TD * n : at + TD * n + TD, :] for ref, at, count in runs for n in range(count)]
    return jnp.concatenate(parts, axis=1)


def stack(parts):
    return jnp.concatenate(parts, axis=0)


def halves(values):
    head = values.astype(BF)
    return jnp.concatenate([head, (values - head.astype(F32)).astype(BF)], axis=1)


def lanes_where(rows, test):
    a = lax.broadcasted_iota(jnp.int32, (rows, 128), 0) % 128
    b = lax.broadcasted_iota(jnp.int32, (rows, 128), 1)
    return test(a, b).astype(F32).astype(BF)


def head_kernel(reps, off_ref, *refs):
    own, mate, x_own, x_mate, y_own, y_mate, far_a, far_b, far_a_mate, far_b_mate, wo_ref = refs[0:11]
    S = (own, mate, x_own, x_mate, y_own, y_mate, far_a, far_a_mate)
    starts = [W_ROWS] * 4 + [2 * W_ROWS] * 2
    x_runs = [[(S[m], at, 4)] for m, at in enumerate(starts)]
    d_runs = [[(S[m], at + TILES, 4)] for m, at in enumerate(starts)]
    for a, b in ((far_a, far_b), (far_a_mate, far_b_mate)):
        x_runs.append([(a, W_ROWS, 1), (b, 0, 3)])
        d_runs.append([(b, 3 * TD, 4)])
    keep_ref, give_ref, w_ref, own_ref, chunks = *refs[11:15], refs[15 : 14 + reps]
    qk_scr, v_scr, acc_scr, g_scr, dq_scr, dvk_scr, dw_scr = refs[14 + reps :]
    me = lax.axis_index("seq")
    chip, core, rep = me // 2, me % 2, lax.axis_index("rep")
    scale = 1.0 / math.sqrt(HD)
    low = low_lanes(TD)
    same_half = lanes_where(256, lambda a, b: (a < HD) == (b < HD))
    low_to_high = lanes_where(256, lambda a, b: (a < HD) & (b >= HD))
    ones_high = lanes_where(TD, lambda a, b: b >= HD)
    blocks = [slice(TD * m, TD * m + TD) for m in range(8)]
    picks = [pl.ds(off_ref[level, me], TD, stride=8) for level in range(2)]

    def spread_high(tile):
        return jnp.where(low, swap_halves(tile), tile)

    for m in range(8):
        rows = pl.ds(pl.multiple_of((me ^ m) * HD, HD), HD)
        w_ref[rows, 0:128] = S[m][pl.ds(pl.multiple_of(core * HD, HD), HD), :]
        w_ref[rows, 128:256] = S[m][2 * HD : W_ROWS, :]
        w_ref[rows, 256:384] = S[m][pl.ds(pl.multiple_of((1 - core) * HD, HD), HD), :]
    x = stack([tiles(*runs) for runs in x_runs])
    upstream = stack([tiles(*runs) for runs in d_runs])
    wide = stack([wo_ref[...], jnp.zeros((HD, DM), BF)])
    da = mm(upstream, wide, NT).astype(BF)
    qkv = mm(x, w_ref[:, 0:256]).astype(BF).astype(F32)
    qk, pair = qkv[:, 0:128], qkv[:, 128:256]
    vv = jnp.where(core == 1, swap_halves(pair), pair)
    rho = lax.rsqrt(mm(halves(qk * qk), same_half) * (1.0 / HD) + 1e-6)
    qkw = qk * rho
    qkn = qkw.astype(BF).astype(F32)
    qk_scr[...] = qkn
    v_scr[...] = vv
    flipped = swap_halves(qkn)

    def forward(qkn, flipped, vv):
        s = mm(qkn[:, :HD].astype(BF), flipped[:, :HD].astype(BF), NT)
        return jnp.exp(s * scale)

    def weigh(e, vv):
        right = stack([jnp.where(low, vv, 1.0).astype(BF), ones_high])
        return mm(halves(e), right)

    near = [forward(qkn[b], flipped[b], vv[b]) for b in blocks]
    for b, e in zip(blocks, near):
        acc_scr[b, :] = weigh(e, vv[b])
    far = [(qk_scr[pick, :], v_scr[pick, :]) for pick in picks]
    far = [(q, swap_halves(q), v) for q, v in far]
    far_e = [forward(*tiles) for tiles in far]
    for pick, e, (_, _, v) in zip(picks, far_e, far):
        acc_scr[pick, :] = acc_scr[pick, :] + weigh(e, v)

    accs = [acc_scr[b, :] for b in blocks]
    rdens = [1.0 / spread_high(acc) for acc in accs]
    attns = [jnp.where(low, acc * r, 0.0).astype(BF) for acc, r in zip(accs, rdens)]
    dot_terms = da.astype(F32) * stack(attns).astype(F32)
    grads = da.astype(F32) + mm(halves(dot_terms), low_to_high)
    g_scr[...] = grads

    def backward(e, rden, flipped, vv, da, delta):
        prob = e * rden
        dp = mm(da, vv.astype(BF), NT)
        ds = (prob * (dp - delta)).astype(BF)
        dq = mm(ds, flipped.astype(BF))
        qz = jnp.where(low, 0.0, flipped).astype(BF)
        return dq, mm(stack([prob.astype(BF), ds]), stack([da, qz]), TN)

    for m, b in enumerate(blocks):
        dq, dvk = backward(
            near[m], rdens[m], flipped[b], vv[b], da[b], spread_high(grads[b])
        )
        dq_scr[b, :] = dq
        dvk_scr[b, :] = dvk
    for pick, e, (_, f, v) in zip(picks, far_e, far):
        g = g_scr[pick, :]
        dq, dvk = backward(
            e,
            1.0 / spread_high(acc_scr[pick, :]),
            f,
            v,
            jnp.where(low, g, 0.0).astype(BF),
            spread_high(g),
        )
        dq_scr[pick, :] = dq_scr[pick, :] + dq
        dvk_scr[pick, :] = dvk_scr[pick, :] + dvk

    low_all = low_lanes(1024)
    dvk = dvk_scr[...]
    dqk = jnp.where(low_all, dq_scr[...], dvk) * scale
    mean = mm(halves(dqk * qkw), same_half) * (1.0 / HD)
    dqk = (rho * (dqk - qkw * mean)).astype(BF)
    attn_high = swap_halves(stack(attns))
    tile = jnp.concatenate([dqk, jnp.where(low_all, dvk, attn_high).astype(BF)], axis=1)
    for m, b in enumerate(blocks):
        ref = give_ref if m % 2 else keep_ref
        ref[TD * (m // 2) : TD * (m // 2) + TD, :] = tile[b]
    dw_scr[0 : 3 * HD, :] = mm(tile[:, 0 : 3 * HD], x, TN)
    dw_scr[3 * HD :, :] = mm(stack(attns), upstream, TN)[:HD]
    for j in range(reps):
        ref = chunks[j - 1] if j else own_ref
        at = pl.multiple_of(((chip ^ rep ^ j) % 4) * TD, TD)
        ref[...] = dw_scr[:, pl.ds(at, 128)].astype(ref.dtype)


def project_kernel(keep_ref, got_ref, w_ref, wo_ref, wo_mate_ref, *outs):
    core = lax.axis_index("seq") % 2
    low = low_lanes(TD)
    wo = jnp.concatenate([wo_ref[...], wo_mate_ref[...]], axis=0)
    for t, out in enumerate(outs):
        rows = slice(TD * t, TD * t + TD)
        a, b = keep_ref[rows, 128:256].astype(F32), got_ref[rows, 128:256].astype(F32)
        attn = jnp.where(low, pltpu.roll(a, HD, 1), b).astype(BF)
        even, odd = jnp.where(core == 1, b, a), jnp.where(core == 1, a, b)
        dv = jnp.where(low, even, pltpu.roll(odd, HD, 1)).astype(BF)
        d_all = jnp.concatenate([keep_ref[rows, 0:128], dv, got_ref[rows, 0:128]], axis=1)
        out[:, 0:DM] = mm(attn, wo).astype(out.dtype)
        out[:, DM:] = mm(d_all, w_ref[...], NT).astype(out.dtype)


def add_kernel(*refs):
    total = refs[0][...].astype(F32)
    for ref in refs[1:-2]:
        total = total + ref[...].astype(F32)
    refs[-2][...] = total[:, 0:DM].astype(BF)
    refs[-1][...] = total[:, DM:].astype(BF)


def sum_kernel(*refs):
    total = refs[0][...]
    for ref in refs[1:-2]:
        total = total + ref[...].astype(F32)
    dv = total[TD : 3 * HD]
    turned = stack([dv, dv]).T
    refs[-2][0:TD, :] = total[0:TD].T.astype(BF)
    refs[-2][TD:, :] = jnp.where(low_lanes(HD), turned[:HD], turned[HD:]).astype(BF)
    refs[-1][...] = total[3 * HD :].astype(BF)


def total_kernel(*refs):
    F, (dw_ref, dwo_ref) = refs[:-2], refs[-2:]
    me = lax.axis_index("seq")
    chip, core = me // 2, me % 2
    rep = lax.axis_index("rep")
    low = low_lanes(HD)
    mine = pl.ds(pl.multiple_of(core * HD, HD), HD)
    for j in range(4):
        col = ((chip ^ rep ^ j) % 4) * 128
        a, b = F[2 * j], F[2 * j + 1]
        aqk, bqk = a[mine, :].astype(F32), b[mine, :].astype(F32)
        av, bv = a[TD : 3 * HD, :].astype(F32), b[TD : 3 * HD, :].astype(F32)
        even, odd = jnp.where(core == 1, bqk, aqk), jnp.where(core == 1, aqk, bqk)
        v = jnp.where(
            low,
            jnp.where(core == 1, pltpu.roll(bv, HD, 1), av),
            jnp.where(core == 1, av, pltpu.roll(bv, HD, 1)),
        )
        tiles = (
            jnp.where(low, even, pltpu.roll(odd, HD, 1)),
            jnp.where(low, pltpu.roll(even, HD, 1), odd),
            v,
        )
        for part, tile in enumerate(tiles):
            dw_ref[:, pl.ds(pl.multiple_of(part * DM + col, 128), 128)] = tile
        dwo_ref[:, pl.ds(pl.multiple_of(col, 128), 128)] = a[3 * HD :, :].astype(F32)


def vmem_call(body, ins, outs, scratch=(), flops=0, smem=0, raw=0):
    bytes_moved = sum(x.size * x.dtype.itemsize for x in list(ins) + list(outs))
    vmem = pl.BlockSpec(memory_space=pltpu.VMEM)
    specs = [pl.BlockSpec(memory_space=pltpu.SMEM)] * smem + [pl.BlockSpec(memory_space=pltpu.HBM)] * raw
    return pl.pallas_call(
        body,
        out_shape=list(outs),
        in_specs=specs + [vmem] * (len(ins) - smem - raw),
        out_specs=[vmem] * len(outs),
        scratch_shapes=list(scratch),
        compiler_params=pltpu.CompilerParams(vmem_limit_bytes=24 << 20),
        cost_estimate=pl.CostEstimate(flops=flops, bytes_accessed=bytes_moved, transcendentals=0),
    )(*ins)


def swap(value, mask, axis):
    return lax.ppermute(value, axis, [(i, i ^ mask) for i in range(lax.axis_size(axis))])


def shape(rows, cols, dtype=BF):
    return jax.ShapeDtypeStruct((rows, cols), dtype)


def after(value, *others):
    return lax.optimization_barrier((value, *others))[0]


def to_owner_chip(value):
    reps, seq = lax.axis_size("rep"), lax.axis_size("seq")
    pairs = [
        ((2 * a + c) * reps + r, (2 * ((a ^ r) % 4) + c) * reps + r)
        for r in range(reps)
        for a in range(seq // 2)
        for c in range(2)
    ]
    return lax.ppermute(value, ("seq", "rep"), pairs)


def local_heads(signal, w_qkv, w_out, offsets, d_result):
    sig, grad = signal[0], d_result[0]
    reps = lax.axis_size("rep")
    pays = vmem_call(
        pack_kernel,
        [pltpu.with_memory_space_constraint(x, pltpu.HBM) for x in (sig, grad, w_qkv)],
        [shape(W_ROWS + 2 * TILES, 128)] * 2 + [shape(2 * W_ROWS + 2 * TILES, 128)],
        scratch=[
            pltpu.VMEM((TD, DM), BF),
            pltpu.VMEM((TD, DM), BF),
            pltpu.VMEM((HD, 3 * DM), BF),
            pltpu.SemaphoreType.DMA((3,)),
        ],
        raw=3,
    )
    x_own = swap(pays[1], 2, "seq")
    y_own = swap(pays[2], 4, "seq")
    far_b = swap(x_own[W_ROWS + TD :], 4, "seq")
    far_a = swap(y_own[W_ROWS : 2 * W_ROWS + TD], 2, "seq")
    S = [pays[0], swap(pays[0], 1, "seq"), x_own, swap(x_own, 1, "seq"), y_own, swap(y_own, 1, "seq")]
    S += [far_a, far_b, swap(far_a, 1, "seq"), swap(after(far_b, far_a), 1, "seq")]
    wo_mate = swap(w_out, 1, "seq")
    scr = [pltpu.VMEM((1024, 128), F32)]
    res = vmem_call(
        functools.partial(head_kernel, reps),
        (offsets, *S, w_out),
        [shape(4 * TD, 256)] * 2
        + [shape(DM, 384), shape(2 * TD, 128, F32)]
        + [shape(2 * TD, 128)] * (reps - 1),
        scratch=scr * 6 + [pltpu.VMEM((256, DM), F32)],
        flops=10**9,
        smem=1,
    )
    keep, give, w_both, own, *chunks = res
    got = swap(give, 1, "seq")
    chunks[0] = after(chunks[0], got)
    arrived = [swap(chunks[j - 1], j, "rep") for j in range(1, reps)]
    Y = vmem_call(
        project_kernel,
        (keep, got, w_both, w_out, wo_mate),
        [shape(TD, 2 * DM, F32)] + [shape(TD, 2 * DM)] * 3,
        flops=5 * 10**8,
    )
    own = after(own, *Y)
    total, dwo_part = vmem_call(
        sum_kernel, (own, *arrived), [shape(3 * HD, 128), shape(HD, 128)]
    )
    Y = [*Y[:3], after(Y[3], total)]
    Y = [Y[0]] + [swap(Y[t], 2 * t, "seq") for t in range(1, 4)]
    result, d_signal = vmem_call(add_kernel, Y, [shape(TD, DM)] * 2)
    rows = jnp.concatenate([to_owner_chip(total), dwo_part], axis=0)
    F = []
    for j in range(reps):
        same = swap(rows, j, "rep") if j else rows
        F += [same, swap(after(same, result) if j == reps - 1 else same, 1, "seq")]
    dw, dwo = vmem_call(
        total_kernel,
        F,
        [shape(HD, 3 * DM, F32), shape(HD, DM, F32)],
    )
    return (result[None], d_signal[None], dw, dwo)


def solution(mesh):
    in_specs = (P("rep", "seq", None), P("seq", None), P("seq", None), P(), P("rep", "seq", None))
    out_specs = (P("rep", "seq", None), P("rep", "seq", None), P("seq", None), P("seq", None))

    def body(signal, w_qkv, w_out, offsets, d_result):
        reps = mesh.shape["rep"]
        per_head = mesh.shape["seq"] == HEADS and reps == 4
        if per_head and signal.shape == (1, TD, DM) and w_qkv.shape == (HD, 3 * DM):
            return local_heads(signal, w_qkv, w_out, offsets, d_result)
        return local(signal, w_qkv, w_out, offsets, d_result)

    return jax.shard_map(body, mesh=mesh, in_specs=in_specs, out_specs=out_specs, check_vma=False)
```

```python
import functools
import math

import jax
import jax.numpy as jnp
from jax import lax
from jax.experimental import pallas as pl
from jax.experimental.pallas import tpu as pltpu
from jax.sharding import PartitionSpec as P

HEADS = 8


def from_partner(value, axis, stride):
    mask = 2**stride
    pairs = [(source, source ^ mask) for source in range(lax.axis_size(axis))]
    return lax.ppermute(value, axis, pairs)


def normalize(tensor):
    widened = tensor.astype(jnp.float32)
    factor = lax.rsqrt(jnp.mean(widened * widened, axis=-1, keepdims=True) + 1e-06)
    return (widened * factor, factor)


def gather_row_subset(full_row_tensor, dilation_step, start_shift):
    row_total = full_row_tensor.shape[0] // dilation_step
    reshaped_tensor = full_row_tensor.reshape(
        row_total, dilation_step, full_row_tensor.shape[1], full_row_tensor.shape[2]
    )
    chosen_rows_list = jnp.arange(dilation_step)[:, None] == start_shift[None, :]
    kept_rows = jnp.where(
        chosen_rows_list[None, :, :, None], reshaped_tensor, jnp.zeros((), full_row_tensor.dtype)
    )
    return jnp.sum(kept_rows, axis=1)


def scatter_row_subset(gathered_rows, dilation_step, start_shift):
    row_total, head_total, feature_count = gathered_rows.shape
    chosen_rows_list = jnp.arange(dilation_step)[:, None] == start_shift[None, :]
    scattered_rows = jnp.where(
        chosen_rows_list[None, :, :, None],
        gathered_rows[:, None],
        jnp.zeros((), gathered_rows.dtype),
    )
    return scattered_rows.reshape(row_total * dilation_step, head_total, feature_count)


def join_halves(own_part, peer_part, upper_bit):
    return jnp.where(
        upper_bit == 1,
        jnp.concatenate([peer_part, own_part], axis=0),
        jnp.concatenate([own_part, peer_part], axis=0),
    )


def attend(query_matrix, key_matrix_rows, value_matrix_rows, logit_scale):
    scores = (
        jnp.einsum(
            "ryk,oyk->yro", query_matrix, key_matrix_rows, preferred_element_type=jnp.float32
        )
        * logit_scale
    )
    exp_scores = jnp.exp(scores)
    softmax_denominator = jnp.sum(exp_scores, axis=-1).T
    softmax_numerator = jnp.einsum(
        "tcg,gto->cto",
        exp_scores.astype(jnp.bfloat16),
        value_matrix_rows,
        preferred_element_type=jnp.float32,
    )
    return (softmax_numerator, softmax_denominator)


def attend_back(
    query_matrix,
    key_matrix_rows,
    value_matrix_rows,
    gradient_rows,
    correction_rows,
    denom_rows,
    logit_scale,
):
    scores = (
        jnp.einsum(
            "ryk,oyk->yro", query_matrix, key_matrix_rows, preferred_element_type=jnp.float32
        )
        * logit_scale
    )
    prob_full = jnp.exp(scores) / denom_rows.T[:, :, None]
    value_gradient = jnp.einsum(
        "jvy,vjk->yjk",
        prob_full.astype(jnp.bfloat16),
        gradient_rows,
        preferred_element_type=jnp.float32,
    )
    probability_gradient = jnp.einsum(
        "ryk,oyk->yro", gradient_rows, value_matrix_rows, preferred_element_type=jnp.float32
    )
    score_gradient = (prob_full * (probability_gradient - correction_rows.T[:, :, None])).astype(
        jnp.bfloat16
    )
    d_query = (
        jnp.einsum(
            "tcg,gto->cto", score_gradient, key_matrix_rows, preferred_element_type=jnp.float32
        )
        * logit_scale
    )
    d_key = (
        jnp.einsum("jvy,vjk->yjk", score_gradient, query_matrix, preferred_element_type=jnp.float32)
        * logit_scale
    )
    return (d_query, d_key, value_gradient)


def local(signal, w_qkv, w_out, offsets, d_result):
    tok_rows = signal[0]
    upstream = d_result[0]
    t_dev, model_dim = tok_rows.shape
    head_total = HEADS
    head_dim = model_dim // head_total
    logit_scale = 1.0 / math.sqrt(head_dim)
    shards = lax.axis_size("seq")
    mid_rate = min(16, shards)
    mid_bits = mid_rate.bit_length() - 1
    shard_index = lax.axis_index("seq")
    mid_off = offsets[0]
    far_off = offsets[1]
    qkv_full, out_full = (
        lax.all_gather(w_qkv, "seq", axis=0, tiled=True),
        lax.all_gather(w_out, "seq", axis=0, tiled=True),
    )
    projected = jnp.dot(tok_rows, qkv_full, preferred_element_type=jnp.float32)
    qkv_rows = projected.astype(jnp.bfloat16)
    query_rows = qkv_rows[:, :model_dim].reshape(t_dev, head_total, head_dim)
    key_matrix_rows = qkv_rows[:, model_dim : 2 * model_dim].reshape(t_dev, head_total, head_dim)
    value_matrix_rows = qkv_rows[:, 2 * model_dim :].reshape(t_dev, head_total, head_dim)
    q_wide, q_factor = normalize(query_rows)
    k_wide, k_factor = normalize(key_matrix_rows)
    query_normalized = q_wide.astype(jnp.bfloat16)
    key_normalized = k_wide.astype(jnp.bfloat16)
    numer_near, denom_near = attend(
        query_normalized, key_normalized, value_matrix_rows, logit_scale
    )
    key_value = jnp.concatenate([key_normalized, value_matrix_rows], axis=2)
    mid_local = gather_row_subset(key_value, mid_rate, mid_off)
    far_local = gather_row_subset(key_value, shards, far_off)
    mid_all = mid_local
    for bit_num in range(mid_bits):
        partner = from_partner(mid_all, "seq", bit_num)
        mid_all = join_halves(mid_all, partner, shard_index // (1 << bit_num) % 2)
    far_all = lax.all_gather(far_local, "seq", axis=0, tiled=True)
    mid_keys_all = mid_all[..., :head_dim]
    mid_vals_all = mid_all[..., head_dim:]
    far_keys_all = far_all[..., :head_dim]
    far_vals_all = far_all[..., head_dim:]
    q_mid = gather_row_subset(query_normalized, mid_rate, mid_off)
    q_far = gather_row_subset(query_normalized, shards, far_off)
    numer_mid, denom_mid = attend(q_mid, mid_keys_all, mid_vals_all, logit_scale)
    numer_far, denom_far = attend(q_far, far_keys_all, far_vals_all, logit_scale)
    softmax_numerator = (
        numer_near
        + scatter_row_subset(numer_mid, mid_rate, mid_off)
        + scatter_row_subset(numer_far, shards, far_off)
    )
    softmax_denominator = (
        denom_near
        + scatter_row_subset(denom_mid[..., None], mid_rate, mid_off)[..., 0]
        + scatter_row_subset(denom_far[..., None], shards, far_off)[..., 0]
    )
    attn_three = (softmax_numerator / softmax_denominator[..., None]).astype(jnp.bfloat16)
    attn_rows = attn_three.reshape(t_dev, model_dim)
    layer_out = jnp.dot(attn_rows, out_full, preferred_element_type=jnp.float32)
    d_attn_wide = jnp.dot(upstream, out_full.T, preferred_element_type=jnp.float32)
    result = layer_out.astype(jnp.bfloat16)
    attention_gradient = d_attn_wide.astype(jnp.bfloat16).reshape(t_dev, head_total, head_dim)
    correction_rows = jnp.sum(
        attention_gradient.astype(jnp.float32) * attn_three.astype(jnp.float32), axis=-1
    )
    dq_near, dk_near, dv_near = attend_back(
        query_normalized,
        key_normalized,
        value_matrix_rows,
        attention_gradient,
        correction_rows,
        softmax_denominator,
        logit_scale,
    )
    g_mid = gather_row_subset(attention_gradient, mid_rate, mid_off)
    g_far = gather_row_subset(attention_gradient, shards, far_off)
    delta_mid = gather_row_subset(correction_rows[..., None], mid_rate, mid_off)[..., 0]
    delta_far = gather_row_subset(correction_rows[..., None], shards, far_off)[..., 0]
    denom_mid_q = gather_row_subset(softmax_denominator[..., None], mid_rate, mid_off)[..., 0]
    denom_far_q = gather_row_subset(softmax_denominator[..., None], shards, far_off)[..., 0]
    dq_mid, dk_mid_part, dv_mid_part = attend_back(
        q_mid, mid_keys_all, mid_vals_all, g_mid, delta_mid, denom_mid_q, logit_scale
    )
    dq_far, dk_far_part, dv_far_part = attend_back(
        q_far, far_keys_all, far_vals_all, g_far, delta_far, denom_far_q, logit_scale
    )
    query_pack = jnp.concatenate([q_mid, g_mid], axis=2)
    stat_pack = jnp.stack([delta_mid, denom_mid_q], axis=2)
    for bit_num in range(mid_bits):
        upper_bit = shard_index // (1 << bit_num) % 2
        peer_query = from_partner(query_pack, "seq", bit_num)
        peer_stats = from_partner(stat_pack, "seq", bit_num)
        query_pack = join_halves(query_pack, peer_query, upper_bit)
        stat_pack = join_halves(stat_pack, peer_stats, upper_bit)
    unused_mid, dk_mid, dv_mid = attend_back(
        query_pack[..., :head_dim],
        mid_local[..., :head_dim],
        mid_local[..., head_dim:],
        query_pack[..., head_dim:],
        stat_pack[..., 0],
        stat_pack[..., 1],
        logit_scale,
    )
    far_query_pack = lax.all_gather(
        jnp.concatenate([q_far, g_far], axis=2), "seq", axis=0, tiled=True
    )
    far_stat_pack = lax.all_gather(
        jnp.stack([delta_far, denom_far_q], axis=2), "seq", axis=0, tiled=True
    )
    unused_far, dk_far, dv_far = attend_back(
        far_query_pack[..., :head_dim],
        far_local[..., :head_dim],
        far_local[..., head_dim:],
        far_query_pack[..., head_dim:],
        far_stat_pack[..., 0],
        far_stat_pack[..., 1],
        logit_scale,
    )
    normed_query_gradient = (
        dq_near
        + scatter_row_subset(dq_mid, mid_rate, mid_off)
        + scatter_row_subset(dq_far, shards, far_off)
    )
    normed_key_gradient = (
        dk_near
        + scatter_row_subset(dk_mid, mid_rate, mid_off)
        + scatter_row_subset(dk_far, shards, far_off)
    )
    value_gradient = (
        dv_near
        + scatter_row_subset(dv_mid, mid_rate, mid_off)
        + scatter_row_subset(dv_far, shards, far_off)
    )
    d_query = q_factor * (
        normed_query_gradient
        - q_wide * jnp.mean(normed_query_gradient * q_wide, axis=-1, keepdims=True)
    )
    d_key = k_factor * (
        normed_key_gradient
        - k_wide * jnp.mean(normed_key_gradient * k_wide, axis=-1, keepdims=True)
    )
    d_qkv = jnp.concatenate(
        [
            d_query.reshape(t_dev, model_dim),
            d_key.reshape(t_dev, model_dim),
            value_gradient.reshape(t_dev, model_dim),
        ],
        axis=1,
    ).astype(jnp.bfloat16)
    d_input = jnp.dot(d_qkv, qkv_full.T, preferred_element_type=jnp.float32)
    d_signal = d_input.astype(jnp.bfloat16)
    grad_in = jnp.einsum("ti,tj->ij", tok_rows, d_qkv, preferred_element_type=jnp.float32)
    grad_mix = jnp.einsum("ti,tj->ij", attn_rows, upstream, preferred_element_type=jnp.float32)
    owned = lax.psum_scatter(
        jnp.concatenate([grad_in, grad_mix], axis=1), "seq", scatter_dimension=0, tiled=True
    )
    owned = lax.psum(owned, "rep")
    return (result[None], d_signal[None], owned[:, : 3 * model_dim], owned[:, 3 * model_dim :])


BF = jnp.bfloat16
F32 = jnp.float32
TD = 128
HD = 64
DM = 512
NN = (((1,), (0,)), ((), ()))
NT = (((1,), (1,)), ((), ()))
TN = (((0,), (0,)), ((), ()))


def mm(a, b, dims=NN):
    return lax.dot_general(a, b, dims, preferred_element_type=F32)


def low_lanes(rows):
    return lax.broadcasted_iota(jnp.int32, (rows, 128), 1) < HD


def swap_halves(tile):
    return pltpu.roll(tile.astype(F32), HD, 1)


W_ROWS = 3 * HD
TILES = 4 * TD


def pack_kernel(sig_ref, grad_ref, wqkv_ref, pay0, pay1, pay2, s_scr, d_scr, w_scr, sems):
    chip = lax.axis_index("seq") // 2
    low = low_lanes(HD)
    loads = [
        pltpu.make_async_copy(src, dst, sems.at[n])
        for n, (src, dst) in enumerate(((wqkv_ref, w_scr), (sig_ref, s_scr), (grad_ref, d_scr)))
    ]
    for load in loads:
        load.start()
    loads[0].wait()
    pays = ((pay0, W_ROWS), (pay1, W_ROWS), (pay2, 2 * W_ROWS))
    for t, (pay, at) in enumerate((*((pay, 0) for pay, _ in pays), (pay2, W_ROWS))):
        col = (chip ^ t) * 128
        q = w_scr[:, pl.ds(pl.multiple_of(col, 128), 128)].astype(F32)
        k = w_scr[:, pl.ds(pl.multiple_of(DM + col, 128), 128)].astype(F32)
        pay[at : at + HD, :] = jnp.where(low, q, swap_halves(k)).astype(BF)
        pay[at + HD : at + 2 * HD, :] = jnp.where(low, swap_halves(q), k).astype(BF)
        pay[at + 2 * HD : at + W_ROWS, :] = w_scr[:, pl.ds(pl.multiple_of(2 * DM + col, 128), 128)]
    for scr, load, shift in ((s_scr, loads[1], 0), (d_scr, loads[2], TILES)):
        load.wait()
        for pay, at in pays:
            for n in range(4):
                row = at + shift + TD * n
                pay[row : row + TD, :] = scr[:, 128 * n : 128 * n + 128]


def tiles(*runs):
    parts = [ref[at + TD * n : at + TD * n + TD, :] for ref, at, count in runs for n in range(count)]
    return jnp.concatenate(parts, axis=1)


def stack(parts):
    return jnp.concatenate(parts, axis=0)


def halves(values):
    head = values.astype(BF)
    return jnp.concatenate([head, (values - head.astype(F32)).astype(BF)], axis=1)


def lanes_where(rows, test):
    a = lax.broadcasted_iota(jnp.int32, (rows, 128), 0) % 128
    b = lax.broadcasted_iota(jnp.int32, (rows, 128), 1)
    return test(a, b).astype(F32).astype(BF)


def head_kernel(reps, off_ref, *refs):
    own, mate, x_own, x_mate, y_own, y_mate, far_a, far_b, far_a_mate, far_b_mate, wo_ref = refs[0:11]
    S = (own, mate, x_own, x_mate, y_own, y_mate, far_a, far_a_mate)
    starts = [W_ROWS] * 4 + [2 * W_ROWS] * 2
    x_runs = [[(S[m], at, 4)] for m, at in enumerate(starts)]
    d_runs = [[(S[m], at + TILES, 4)] for m, at in enumerate(starts)]
    for a, b in ((far_a, far_b), (far_a_mate, far_b_mate)):
        x_runs.append([(a, W_ROWS, 1), (b, 0, 3)])
        d_runs.append([(b, 3 * TD, 4)])
    keep_ref, give_ref, w_ref, own_ref, chunks = *refs[11:15], refs[15 : 14 + reps]
    qk_scr, v_scr, acc_scr, g_scr, dq_scr, dvk_scr, dw_scr = refs[14 + reps :]
    me = lax.axis_index("seq")
    chip, core, rep = me // 2, me % 2, lax.axis_index("rep")
    scale = 1.0 / math.sqrt(HD)
    low = low_lanes(TD)
    same_half = lanes_where(256, lambda a, b: (a < HD) == (b < HD))
    low_to_high = lanes_where(256, lambda a, b: (a < HD) & (b >= HD))
    ones_high = lanes_where(TD, lambda a, b: b >= HD)
    blocks = [slice(TD * m, TD * m + TD) for m in range(8)]
    picks = [pl.ds(off_ref[level, me], TD, stride=8) for level in range(2)]

    def spread_high(tile):
        return jnp.where(low, swap_halves(tile), tile)

    for m in range(8):
        rows = pl.ds(pl.multiple_of((me ^ m) * HD, HD), HD)
        w_ref[rows, 0:128] = S[m][pl.ds(pl.multiple_of(core * HD, HD), HD), :]
        w_ref[rows, 128:256] = S[m][2 * HD : W_ROWS, :]
        w_ref[rows, 256:384] = S[m][pl.ds(pl.multiple_of((1 - core) * HD, HD), HD), :]
    x = stack([tiles(*runs) for runs in x_runs])
    upstream = stack([tiles(*runs) for runs in d_runs])
    wide = stack([wo_ref[...], jnp.zeros((HD, DM), BF)])
    da = mm(upstream, wide, NT).astype(BF)
    qkv = mm(x, w_ref[:, 0:256]).astype(BF).astype(F32)
    qk, pair = qkv[:, 0:128], qkv[:, 128:256]
    vv = jnp.where(core == 1, swap_halves(pair), pair)
    rho = lax.rsqrt(mm(halves(qk * qk), same_half) * (1.0 / HD) + 1e-6)
    qkw = qk * rho
    qkn = qkw.astype(BF).astype(F32)
    qk_scr[...] = qkn
    v_scr[...] = vv
    flipped = swap_halves(qkn)

    def forward(qkn, flipped, vv):
        s = mm(qkn[:, :HD].astype(BF), flipped[:, :HD].astype(BF), NT)
        return jnp.exp(s * scale)

    def weigh(e, vv):
        right = stack([jnp.where(low, vv, 1.0).astype(BF), ones_high])
        return mm(halves(e), right)

    near = [forward(qkn[b], flipped[b], vv[b]) for b in blocks]
    for b, e in zip(blocks, near):
        acc_scr[b, :] = weigh(e, vv[b])
    far = [(qk_scr[pick, :], v_scr[pick, :]) for pick in picks]
    far = [(q, swap_halves(q), v) for q, v in far]
    far_e = [forward(*tiles) for tiles in far]
    for pick, e, (_, _, v) in zip(picks, far_e, far):
        acc_scr[pick, :] = acc_scr[pick, :] + weigh(e, v)

    accs = [acc_scr[b, :] for b in blocks]
    rdens = [1.0 / spread_high(acc) for acc in accs]
    attns = [jnp.where(low, acc * r, 0.0).astype(BF) for acc, r in zip(accs, rdens)]
    dot_terms = da.astype(F32) * stack(attns).astype(F32)
    grads = da.astype(F32) + mm(halves(dot_terms), low_to_high)
    g_scr[...] = grads

    def backward(e, rden, flipped, vv, da, delta):
        prob = e * rden
        dp = mm(da, vv.astype(BF), NT)
        ds = (prob * (dp - delta)).astype(BF)
        dq = mm(ds, flipped.astype(BF))
        qz = jnp.where(low, 0.0, flipped).astype(BF)
        return dq, mm(stack([prob.astype(BF), ds]), stack([da, qz]), TN)

    for m, b in enumerate(blocks):
        dq, dvk = backward(
            near[m], rdens[m], flipped[b], vv[b], da[b], spread_high(grads[b])
        )
        dq_scr[b, :] = dq
        dvk_scr[b, :] = dvk
    for pick, e, (_, f, v) in zip(picks, far_e, far):
        g = g_scr[pick, :]
        dq, dvk = backward(
            e,
            1.0 / spread_high(acc_scr[pick, :]),
            f,
            v,
            jnp.where(low, g, 0.0).astype(BF),
            spread_high(g),
        )
        dq_scr[pick, :] = dq_scr[pick, :] + dq
        dvk_scr[pick, :] = dvk_scr[pick, :] + dvk

    low_all = low_lanes(1024)
    dvk = dvk_scr[...]
    dqk = jnp.where(low_all, dq_scr[...], dvk) * scale
    mean = mm(halves(dqk * qkw), same_half) * (1.0 / HD)
    dqk = (rho * (dqk - qkw * mean)).astype(BF)
    attn_high = swap_halves(stack(attns))
    tile = jnp.concatenate([dqk, jnp.where(low_all, dvk, attn_high).astype(BF)], axis=1)
    for m, b in enumerate(blocks):
        ref = give_ref if m % 2 else keep_ref
        ref[TD * (m // 2) : TD * (m // 2) + TD, :] = tile[b]
    dw_scr[0 : 3 * HD, :] = mm(tile[:, 0 : 3 * HD], x, TN)
    dw_scr[3 * HD :, :] = mm(stack(attns), upstream, TN)[:HD]
    for j in range(reps):
        ref = chunks[j - 1] if j else own_ref
        at = pl.multiple_of(((chip ^ rep ^ j) % 4) * TD, TD)
        ref[...] = dw_scr[:, pl.ds(at, 128)].astype(ref.dtype)


def project_kernel(keep_ref, got_ref, w_ref, wo_ref, wo_mate_ref, *outs):
    core = lax.axis_index("seq") % 2
    low = low_lanes(TD)
    wo = jnp.concatenate([wo_ref[...], wo_mate_ref[...]], axis=0)
    for t, out in enumerate(outs):
        rows = slice(TD * t, TD * t + TD)
        a, b = keep_ref[rows, 128:256].astype(F32), got_ref[rows, 128:256].astype(F32)
        attn = jnp.where(low, pltpu.roll(a, HD, 1), b).astype(BF)
        even, odd = jnp.where(core == 1, b, a), jnp.where(core == 1, a, b)
        dv = jnp.where(low, even, pltpu.roll(odd, HD, 1)).astype(BF)
        d_all = jnp.concatenate([keep_ref[rows, 0:128], dv, got_ref[rows, 0:128]], axis=1)
        out[:, 0:DM] = mm(attn, wo).astype(out.dtype)
        out[:, DM:] = mm(d_all, w_ref[...], NT).astype(out.dtype)


def add_kernel(*refs):
    total = refs[0][...].astype(F32)
    for ref in refs[1:-2]:
        total = total + ref[...].astype(F32)
    refs[-2][...] = total[:, 0:DM].astype(BF)
    refs[-1][...] = total[:, DM:].astype(BF)


def sum_kernel(*refs):
    total = refs[0][...]
    for ref in refs[1:-2]:
        total = total + ref[...].astype(F32)
    dv = total[TD : 3 * HD]
    turned = stack([dv, dv]).T
    refs[-2][0:TD, :] = total[0:TD].T.astype(BF)
    refs[-2][TD:, :] = jnp.where(low_lanes(HD), turned[:HD], turned[HD:]).astype(BF)
    refs[-1][...] = total[3 * HD :].astype(BF)


def total_kernel(*refs):
    F, (dw_ref, dwo_ref) = refs[:-2], refs[-2:]
    me = lax.axis_index("seq")
    chip, core = me // 2, me % 2
    rep = lax.axis_index("rep")
    low = low_lanes(HD)
    mine = pl.ds(pl.multiple_of(core * HD, HD), HD)
    for j in range(4):
        col = ((chip ^ rep ^ j) % 4) * 128
        a, b = F[2 * j], F[2 * j + 1]
        aqk, bqk = a[mine, :].astype(F32), b[mine, :].astype(F32)
        av, bv = a[TD : 3 * HD, :].astype(F32), b[TD : 3 * HD, :].astype(F32)
        even, odd = jnp.where(core == 1, bqk, aqk), jnp.where(core == 1, aqk, bqk)
        v = jnp.where(
            low,
            jnp.where(core == 1, pltpu.roll(bv, HD, 1), av),
            jnp.where(core == 1, av, pltpu.roll(bv, HD, 1)),
        )
        tiles = (
            jnp.where(low, even, pltpu.roll(odd, HD, 1)),
            jnp.where(low, pltpu.roll(even, HD, 1), odd),
            v,
        )
        for part, tile in enumerate(tiles):
            dw_ref[:, pl.ds(pl.multiple_of(part * DM + col, 128), 128)] = tile
        dwo_ref[:, pl.ds(pl.multiple_of(col, 128), 128)] = a[3 * HD :, :].astype(F32)


def vmem_call(body, ins, outs, scratch=(), flops=0, smem=0, raw=0):
    bytes_moved = sum(x.size * x.dtype.itemsize for x in list(ins) + list(outs))
    vmem = pl.BlockSpec(memory_space=pltpu.VMEM)
    specs = [pl.BlockSpec(memory_space=pltpu.SMEM)] * smem + [pl.BlockSpec(memory_space=pltpu.HBM)] * raw
    return pl.pallas_call(
        body,
        out_shape=list(outs),
        in_specs=specs + [vmem] * (len(ins) - smem - raw),
        out_specs=[vmem] * len(outs),
        scratch_shapes=list(scratch),
        compiler_params=pltpu.CompilerParams(vmem_limit_bytes=24 << 20),
        cost_estimate=pl.CostEstimate(flops=flops, bytes_accessed=bytes_moved, transcendentals=0),
    )(*ins)


def swap(value, mask, axis):
    return lax.ppermute(value, axis, [(i, i ^ mask) for i in range(lax.axis_size(axis))])


def shape(rows, cols, dtype=BF):
    return jax.ShapeDtypeStruct((rows, cols), dtype)


def after(value, *others):
    return lax.optimization_barrier((value, *others))[0]


def to_owner_chip(value):
    reps, seq = lax.axis_size("rep"), lax.axis_size("seq")
    pairs = [
        ((2 * a + c) * reps + r, (2 * ((a ^ r) % 4) + c) * reps + r)
        for r in range(reps)
        for a in range(seq // 2)
        for c in range(2)
    ]
    return lax.ppermute(value, ("seq", "rep"), pairs)


def local_heads(signal, w_qkv, w_out, offsets, d_result):
    sig, grad = signal[0], d_result[0]
    reps = lax.axis_size("rep")
    pays = vmem_call(
        pack_kernel,
        [pltpu.with_memory_space_constraint(x, pltpu.HBM) for x in (sig, grad, w_qkv)],
        [shape(W_ROWS + 2 * TILES, 128)] * 2 + [shape(2 * W_ROWS + 2 * TILES, 128)],
        scratch=[
            pltpu.VMEM((TD, DM), BF),
            pltpu.VMEM((TD, DM), BF),
            pltpu.VMEM((HD, 3 * DM), BF),
            pltpu.SemaphoreType.DMA((3,)),
        ],
        raw=3,
    )
    x_own = swap(pays[1], 2, "seq")
    y_own = swap(pays[2], 4, "seq")
    far_b = swap(x_own[W_ROWS + TD :], 4, "seq")
    far_a = swap(y_own[W_ROWS : 2 * W_ROWS + TD], 2, "seq")
    S = [pays[0], swap(pays[0], 1, "seq"), x_own, swap(x_own, 1, "seq"), y_own, swap(y_own, 1, "seq")]
    S += [far_a, far_b, swap(far_a, 1, "seq"), swap(after(far_b, far_a), 1, "seq")]
    wo_mate = swap(w_out, 1, "seq")
    scr = [pltpu.VMEM((1024, 128), F32)]
    res = vmem_call(
        functools.partial(head_kernel, reps),
        (offsets, *S, w_out),
        [shape(4 * TD, 256)] * 2
        + [shape(DM, 384), shape(2 * TD, 128, F32)]
        + [shape(2 * TD, 128)] * (reps - 1),
        scratch=scr * 6 + [pltpu.VMEM((256, DM), F32)],
        flops=10**9,
        smem=1,
    )
    keep, give, w_both, own, *chunks = res
    got = swap(give, 1, "seq")
    chunks[0] = after(chunks[0], got)
    arrived = [swap(chunks[j - 1], j, "rep") for j in range(1, reps)]
    Y = vmem_call(
        project_kernel,
        (keep, got, w_both, w_out, wo_mate),
        [shape(TD, 2 * DM, F32)] + [shape(TD, 2 * DM)] * 3,
        flops=5 * 10**8,
    )
    own = after(own, *Y)
    total, dwo_part = vmem_call(
        sum_kernel, (own, *arrived), [shape(3 * HD, 128), shape(HD, 128)]
    )
    Y = [*Y[:3], after(Y[3], total)]
    Y = [Y[0]] + [swap(Y[t], 2 * t, "seq") for t in range(1, 4)]
    result, d_signal = vmem_call(add_kernel, Y, [shape(TD, DM)] * 2)
    rows = jnp.concatenate([to_owner_chip(total), dwo_part], axis=0)
    F = [None] * reps
    for j in (3, 2, 1, 0):
        same = swap(rows, j, "rep") if j else rows
        F[j] = [same, swap(after(same, result) if j == 2 else same, 1, "seq")]
    F = sum(F, [])
    dw, dwo = vmem_call(
        total_kernel,
        F,
        [shape(HD, 3 * DM, F32), shape(HD, DM, F32)],
    )
    return (result[None], d_signal[None], dw, dwo)


def solution(mesh):
    in_specs = (P("rep", "seq", None), P("seq", None), P("seq", None), P(), P("rep", "seq", None))
    out_specs = (P("rep", "seq", None), P("rep", "seq", None), P("seq", None), P("seq", None))

    def body(signal, w_qkv, w_out, offsets, d_result):
        reps = mesh.shape["rep"]
        per_head = mesh.shape["seq"] == HEADS and reps == 4
        if per_head and signal.shape == (1, TD, DM) and w_qkv.shape == (HD, 3 * DM):
            return local_heads(signal, w_qkv, w_out, offsets, d_result)
        return local(signal, w_qkv, w_out, offsets, d_result)

    return jax.shard_map(body, mesh=mesh, in_specs=in_specs, out_specs=out_specs, check_vma=False)
```
